32 devices in a mesh: dp: 4 (over z), row: 4 (over y, x), col: 2 (over core).
Axes of the slice: x: 2, y: 2, z: 4, core: 2. Of those that a mesh axis runs over, the one named last changes fastest.
Arguments:
- grad_parts: bfloat16 [4, 1, 4, 512, 10240], P('dp', None, 'row', None, 'col'), may hold values from -6 to 6
- params: float32 [1, 4, 512, 10240], P(None, 'row', 'dp', 'col'), may hold values from -6 to 6
- row_second: float32 [1, 4, 512], P(None, 'row'), may hold values from 0.1 to 90
- col_second: float32 [1, 10240], P(None, 'col'), may hold values from 0.02 to 100
Outputs:
- new_params: float32 [1, 4, 512, 10240], P(None, 'row', 'dp', 'col')
- new_row: float32 [1, 4, 512], P(None, 'row', 'dp')
- new_col: float32 [1, 10240], P(None, 'col')
The draws below stay inside these ranges and needn't reach their ends.
All inputs are finite; a program needn't handle non-finite values.
Results may differ from the reference program's by a relative error of at most 0.0003.
Values sent between devices are 32-bit elements; how exact they have to be, the bound alone decides.
No kernel may reach another device: no remote copies, remote signals or barrier semaphores. Data moves between devices by JAX's collectives and lax.ppermute only.
A program may use at most 64 MiB of HBM per device.

```python
import math
import jax
import jax.numpy as jnp
from jax import lax

ROWS = 2048
FF = 10240
LAYERS = 1
SLAB = 512
N_DP = 4
N_ROW = 4


def heavy_columns(key):
    block_order = jax.random.permutation(jax.random.fold_in(key, 11), 4)
    chosen = (block_order < 2).astype(jnp.float32)
    column_block = jnp.arange(FF) * 4 // FF
    return chosen[column_block]


def draw_grad_parts(key, part):
    heavy = heavy_columns(key)
    upper_rows = (jnp.arange(SLAB) >= SLAB // 2).astype(jnp.float32)
    matched = upper_rows[:, None] * heavy[None, :] + (1.0 - upper_rows[:, None]) * (1.0 - heavy[None, :])
    interact = 1.0 + 0.8 * matched
    row_scale = jnp.exp(jax.random.uniform(jax.random.fold_in(key, 21), (N_ROW, SLAB), jnp.float32, -0.6, 0.6))
    col_scale = jnp.exp(jax.random.uniform(jax.random.fold_in(key, 22), (FF,), jnp.float32, -0.6, 0.6))
    amplitude = interact[None, :, :] * row_scale[:, :, None] * col_scale[None, None, :]
    shape_all = (N_DP, LAYERS, N_ROW, SLAB, FF)
    random_part = jnp.clip(jax.random.normal(jax.random.fold_in(key, 23), shape_all, jnp.float32), -4.0, 4.0)
    return (0.25 * random_part * amplitude[None, None, :, :, :]).astype(jnp.bfloat16)


def draw_row_second(key, part):
    position = jnp.arange(SLAB, dtype=jnp.float32) / SLAB
    rising = jnp.power(10.0, position)
    exponent = jax.random.uniform(key, (LAYERS, N_ROW, SLAB), jnp.float32, math.log(0.1), math.log(0.3))
    return jnp.exp(exponent) * rising[None, None, :]


def draw_col_second(key, part):
    heavy = heavy_columns(key)
    odd_layer = (jnp.arange(LAYERS) % 2).astype(jnp.float32)
    small_part = jnp.exp(jax.random.uniform(jax.random.fold_in(key, 31), (LAYERS, FF), jnp.float32, math.log(0.02), math.log(0.2)))
    small_part = small_part * (1.0 + 29.0 * heavy)[None, :]
    large_part = jnp.exp(jax.random.uniform(jax.random.fold_in(key, 32), (LAYERS, FF), jnp.float32, math.log(10.0), math.log(100.0)))
    return small_part * (1.0 - odd_layer)[:, None] + large_part * odd_layer[:, None]


def levels(own_key, extent, shards, smallest, top_value):
    gain = 1.0
    for dim, parts in shards:
        draws = jax.random.uniform(jax.random.fold_in(jax.random.fold_in(own_key, 6), dim), (parts,), jnp.float32, smallest / len(shards), top_value / len(shards))
        gain = gain * jnp.repeat(jnp.exp(draws), extent[dim] // parts).reshape((-1,) + (1,) * (len(extent) - 1 - dim))
    return gain


def normal_values(rng, shape, width, reach, pieces=(), held_as=jnp.bfloat16):
    entries = width * jax.random.normal(rng, shape, jnp.float32)
    if pieces:
        entries = entries * levels(rng, shape, pieces, -0.22, 0.18)
    return jnp.clip(entries, -reach, reach).astype(held_as)


def setup_inputs(seed: int = 0) -> dict:
    key_of = jax.random.split(jax.random.key(seed), 5)
    grad_parts = draw_grad_parts(jax.random.fold_in(key_of[4], 71), 0)
    params = normal_values(key_of[1], (LAYERS, N_ROW, SLAB, FF), 1.0, 6.0, ((1, 4), (2, 4), (3, 2)), jnp.float32)
    row_second = draw_row_second(jax.random.fold_in(key_of[4], 71), 0)
    col_second = draw_col_second(jax.random.fold_in(key_of[4], 71), 0)
    return dict(grad_parts=grad_parts, params=params, row_second=row_second, col_second=col_second)


beta_two = 1.0 - 8.0 ** (-0.8)
step_rate = 0.5
tiny_add = 1e-30

def reference(grad_parts, params, row_second, col_second):
    summed_grad = jnp.zeros(params.shape, jnp.float32)
    for replica in range(N_DP):
        summed_grad = summed_grad + grad_parts[replica].astype(jnp.float32)
    gradient = summed_grad.reshape(LAYERS, ROWS, FF)
    weights = params.reshape(LAYERS, ROWS, FF)
    old_rows = row_second.reshape(LAYERS, ROWS)
    squares = gradient * gradient + tiny_add
    new_row = beta_two * old_rows + (1.0 - beta_two) * lax.optimization_barrier(jnp.mean(squares, axis=2))
    new_col = beta_two * col_second + (1.0 - beta_two) * lax.optimization_barrier(jnp.mean(squares, axis=1))
    row_mean = lax.optimization_barrier(jnp.mean(new_row, axis=1))
    denominator = new_row[:, :, None] * new_col[:, None, :] / row_mean[:, None, None]
    update = gradient * lax.rsqrt(denominator)
    clip_ratio = jnp.sqrt(lax.optimization_barrier(jnp.mean(update * update, axis=(1, 2))))
    new_params = weights - step_rate * update / jnp.maximum(1.0, clip_ratio)[:, None, None]
    return (new_params.reshape(LAYERS, N_ROW, SLAB, FF), new_row.reshape(LAYERS, N_ROW, SLAB), new_col)
```

```python
import jax
import jax.numpy as jnp
from jax import lax
from jax.sharding import PartitionSpec as P

beta_two = 1.0 - 8.0 ** (-0.8)
step_rate = 0.5
tiny_add = 1e-30
pieces = 4


def axis_sum(values, axis):
    size = lax.axis_size(axis)
    hop = 1
    while hop < size:
        pairs = [(i, i ^ hop) for i in range(size)]
        values = values + lax.ppermute(values, axis, pairs)
        hop *= 2
    return values


def shards(grad_parts, params, row_second, col_second):
    owned_rows = params.shape[2]
    local_cols = params.shape[3]
    slab_rows = row_second.shape[2]
    hidden_width = local_cols * lax.axis_size("col")
    matrix_rows = slab_rows * lax.axis_size("row")
    replicas = lax.axis_size("dp")
    place = lax.axis_index("dp")
    piece_rows = owned_rows // pieces
    grad_local = grad_parts.reshape(slab_rows, local_cols)
    weights = params.reshape(owned_rows, local_cols)
    old_rows = lax.dynamic_slice_in_dim(row_second.reshape(slab_rows, 1), place * owned_rows, owned_rows, 0)
    old_cols = col_second.reshape(1, local_cols)

    def own(owner, piece):
        start = jnp.clip(owner, 0, replicas - 1) * owned_rows + piece * piece_rows
        return lax.dynamic_slice_in_dim(grad_local, start, piece_rows, 0).astype(jnp.float32)

    from_left = [None] * pieces
    from_right = [None] * pieces
    for step in range(replicas - 1):
        to_right = [(i, i + 1) for i in range(step + 1)]
        to_left = [(replicas - 1 - i, replicas - 2 - i) for i in range(step + 1)]
        for piece in range(pieces):
            right = own(replicas - 1 - step + place, piece)
            left = own(step - (replicas - 1) + place, piece)
            if step > 0:
                right = right + from_left[piece]
                left = left + from_right[piece]
            from_left[piece] = lax.ppermute(right, "dp", to_right)
            from_right[piece] = lax.ppermute(left, "dp", to_left)

    gradient = []
    new_row = []
    col_part = 0.0
    scaled_part = 0.0
    for piece in range(pieces):
        grad_piece = own(place, piece) + from_left[piece] + from_right[piece]
        squares = grad_piece * grad_piece + tiny_add
        row_sum = axis_sum(jnp.sum(squares, axis=1, keepdims=True), "col")
        old_piece = old_rows[piece * piece_rows : (piece + 1) * piece_rows]
        row_piece = beta_two * old_piece + (1.0 - beta_two) * (row_sum / hidden_width)
        col_part = col_part + jnp.sum(squares, axis=0, keepdims=True)
        scaled_part = scaled_part + jnp.sum(grad_piece * grad_piece / row_piece, axis=0, keepdims=True)
        gradient.append(grad_piece)
        new_row.append(row_piece)
    new_row = jnp.concatenate(new_row, axis=0)
    row_part = jnp.broadcast_to(jnp.sum(new_row), (1, 128))
    packed = jnp.concatenate([col_part, scaled_part, row_part], axis=1)
    packed = axis_sum(axis_sum(packed, "row"), "dp")
    col_sum = packed[:, :local_cols]
    scaled_sum = packed[:, local_cols : 2 * local_cols]
    row_mean = packed[0, 2 * local_cols] / matrix_rows
    new_col = beta_two * old_cols + (1.0 - beta_two) * (col_sum / matrix_rows)
    update_part = jnp.broadcast_to(jnp.sum(scaled_sum / new_col), (1, 128))
    update_total = axis_sum(update_part, "col")[0, 0] * row_mean
    clip_ratio = jnp.sqrt(update_total / (matrix_rows * hidden_width))
    factor = step_rate * jnp.sqrt(row_mean) / jnp.maximum(1.0, clip_ratio)
    row_scale = lax.rsqrt(new_row)
    col_scale = factor * lax.rsqrt(new_col)
    new_params = weights - jnp.concatenate(gradient, axis=0) * row_scale * col_scale
    return (new_params.reshape(params.shape), new_row.reshape(1, 1, owned_rows), new_col)


def solution(mesh):
    return jax.shard_map(
        shards,
        mesh=mesh,
        in_specs=(
            P("dp", None, "row", None, "col"),
            P(None, "row", "dp", "col"),
            P(None, "row", None),
            P(None, "col"),
        ),
        out_specs=(P(None, "row", "dp", "col"), P(None, "row", "dp"), P(None, "col")),
        check_vma=False,
    )
```

```python
import jax
import jax.numpy as jnp
from jax import lax
from jax.experimental import pallas as pl
from jax.experimental.pallas import tpu as pltpu
from jax.sharding import PartitionSpec as P

beta_two = 1.0 - 8.0 ** (-0.8)
step_rate = 0.5
tiny_add = 1e-30
lanes = 128
in_flight = 2
ON_CHIP = pl.BlockSpec(memory_space=pltpu.VMEM)
IN_PLACE = pl.BlockSpec(memory_space=pl.ANY)
limits = pltpu.CompilerParams(vmem_limit_bytes=32 * 1024 * 1024)


def f32(*shape):
    return jax.ShapeDtypeStruct(shape, jnp.float32)


def cost(elements, flops, width):
    return pl.CostEstimate(flops=flops * elements, bytes_accessed=width * elements, transcendentals=0)


def axis_sum(values, axis):
    size = lax.axis_size(axis)
    hop = 1
    while hop < size:
        pairs = [(i, i ^ hop) for i in range(size)]
        values = values + lax.ppermute(values, axis, pairs)
        hop *= 2
    return values


def other_parts(values, axis):
    size = lax.axis_size(axis)
    return [lax.ppermute(values, axis, [(i, (i + k) % size) for i in range(size)]) for k in range(1, size)]


def make_partials(grad, arrived, tokens, owners, replicas, pieces, piece, rows):
    cols = grad.shape[1]

    def body(grad_ref, *refs):
        right_out, left_out, right_own, left_own, sems = refs[-5:]
        place = lax.axis_index("dp")
        copies = []
        for k, own in enumerate((right_own, left_own)):
            owner = jnp.clip(place + owners[k], 0, replicas - 1)
            start = pl.multiple_of((owner * pieces + piece) * rows, rows)
            copies.append(pltpu.make_async_copy(grad_ref.at[pl.ds(start, rows), :], own, sems.at[k]))
            copies[-1].start()
        for k, out in enumerate((right_out, left_out)):
            copies[k].wait()
            values = (right_own, left_own)[k][...].astype(jnp.float32)
            if arrived:
                values = values + refs[k][...]
            out[...] = values

    return pl.pallas_call(
        body,
        out_shape=(f32(rows, cols), f32(rows, cols)),
        in_specs=[IN_PLACE] + [ON_CHIP] * (len(arrived) + len(tokens)),
        out_specs=(ON_CHIP, ON_CHIP),
        scratch_shapes=[
            pltpu.VMEM((rows, cols), grad.dtype),
            pltpu.VMEM((rows, cols), grad.dtype),
            pltpu.SemaphoreType.DMA((2,)),
        ],
        compiler_params=limits,
        cost_estimate=cost(rows * cols, 2, 20),
        name="partials",
    )(grad, *arrived, *tokens)


def finish_piece(own, arrived, tokens, piece, rows):
    cols = own.shape[1]

    def body(own_ref, left_ref, right_ref, *refs):
        grad_ref, row_ref, col_ref = refs[-3:]
        for k in range(cols // lanes):
            at = pl.ds(k * lanes, lanes)
            values = own_ref[piece * rows : (piece + 1) * rows, at].astype(jnp.float32)
            values = values + left_ref[:, at] + right_ref[:, at]
            grad_ref[:, at] = values
            squares = values * values + tiny_add
            row_part = squares if k == 0 else row_part + squares
            col_ref[:, at] = jnp.sum(squares, axis=0, keepdims=True)
        row_ref[...] = row_part

    return pl.pallas_call(
        body,
        out_shape=(f32(rows, cols), f32(rows, lanes), f32(1, cols)),
        in_specs=[ON_CHIP] * (3 + len(tokens)),
        out_specs=(ON_CHIP,) * 3,
        compiler_params=limits,
        cost_estimate=cost(rows * cols, 6, 14),
        name="finish",
    )(own, *arrived, *tokens)


def scale_piece(gradient, row_parts, old_rows, col_part, before, hidden_width, piece, rows):
    cols = gradient.shape[1]
    held = [] if before is None else [before]

    def body(grad_ref, col_ref, old_ref, *refs):
        row_out, sums_out = refs[-2:]
        total = refs[0][...]
        for ref in refs[1 : len(row_parts)]:
            total = total + ref[...]
        row_sum = jnp.sum(total, axis=1, keepdims=True)
        old = old_ref[piece * rows : (piece + 1) * rows, :]
        row = beta_two * old + (1.0 - beta_two) * (row_sum / hidden_width)
        row_out[...] = row
        inverse = 1.0 / row
        row_total = jnp.sum(row, axis=0, keepdims=True)
        end = pl.ds(2 * cols, lanes)
        sums_out[:, end] = refs[len(row_parts)][:, end] + row_total if held else row_total
        for k in range(cols // lanes):
            at = pl.ds(k * lanes, lanes)
            after = pl.ds(cols + k * lanes, lanes)
            values = grad_ref[:, at]
            scaled = jnp.sum(values * values * inverse, axis=0, keepdims=True)
            col = col_ref[:, at]
            if held:
                col = col + refs[len(row_parts)][:, at]
                scaled = scaled + refs[len(row_parts)][:, after]
            sums_out[:, at] = col
            sums_out[:, after] = scaled

    return pl.pallas_call(
        body,
        out_shape=(f32(rows, lanes), f32(1, 2 * cols + lanes)),
        in_specs=[ON_CHIP] * (3 + len(row_parts) + len(held)),
        out_specs=(ON_CHIP, ON_CHIP),
        compiler_params=limits,
        cost_estimate=cost(rows * cols, 4, 4),
        name="scale",
    )(gradient, col_part, old_rows, *row_parts, *held)


def column_factor(sums, old_cols, matrix_rows):
    cols = old_cols.shape[1]

    def body(sums_ref, old_ref, col_out, update_out):
        col = beta_two * old_ref[...] + (1.0 - beta_two) * (sums_ref[:, :cols] / matrix_rows)
        col_out[...] = col
        ratio = sums_ref[:, cols : 2 * cols] / col
        total = ratio[:, :lanes]
        for k in range(1, cols // lanes):
            total = total + ratio[:, k * lanes : (k + 1) * lanes]
        update_out[...] = total

    return pl.pallas_call(
        body,
        out_shape=(f32(1, cols), f32(1, lanes)),
        in_specs=[ON_CHIP] * 2,
        out_specs=(ON_CHIP, ON_CHIP),
        compiler_params=limits,
        cost_estimate=cost(cols, 4, 12),
        name="columns",
    )(sums, old_cols)


def apply_update(weights, gradient, new_row, new_col, sums, updates, matrix_rows, hidden_width):
    rows, cols = gradient[0].shape
    count = len(gradient)

    def body(weights_ref, col_ref, sums_ref, *refs):
        grad_refs = refs[:count]
        row_refs = refs[count : 2 * count]
        update_refs = refs[2 * count : 2 * count + len(updates)]
        out_ref, held, sems = refs[-3:]
        update_total = update_refs[0][...]
        for ref in update_refs[1:]:
            update_total = update_total + ref[...]
        update_total = jnp.sum(update_total, axis=1, keepdims=True)
        row_mean = sums_ref[:, 2 * cols : 2 * cols + 1] / matrix_rows
        clip_ratio = jnp.sqrt(update_total * row_mean / (matrix_rows * hidden_width))
        factor = step_rate * jnp.sqrt(row_mean) / jnp.maximum(1.0, clip_ratio)
        col_scale = factor * lax.rsqrt(col_ref[...])
        copies = []
        for k in range(count):
            here = slice(k * rows, (k + 1) * rows)
            row_scale = lax.rsqrt(row_refs[k][:, :1])
            held[here, :] = weights_ref[here, :] - grad_refs[k][...] * row_scale * col_scale
            copies.append(pltpu.make_async_copy(held.at[here, :], out_ref.at[here, :], sems.at[k]))
            copies[-1].start()
        for copy in copies:
            copy.wait()

    return pl.pallas_call(
        body,
        out_shape=f32(rows * count, cols),
        in_specs=[ON_CHIP] * (3 + 2 * count + len(updates)),
        out_specs=IN_PLACE,
        scratch_shapes=[pltpu.VMEM((rows * count, cols), jnp.float32), pltpu.SemaphoreType.DMA((count,))],
        compiler_params=limits,
        cost_estimate=cost(rows * count * cols, 4, 12),
        name="apply",
    )(weights, new_col, sums, *gradient, *new_row, *updates)


def shards(grad_parts, params, row_second, col_second):
    owned_rows = params.shape[2]
    local_cols = params.shape[3]
    slab_rows = row_second.shape[2]
    hidden_width = local_cols * lax.axis_size("col")
    matrix_rows = slab_rows * lax.axis_size("row")
    replicas = lax.axis_size("dp")
    first_row = lax.axis_index("dp") * owned_rows
    pieces = max(1, min(4, owned_rows // 16))
    piece_rows = owned_rows // pieces
    grad = grad_parts.reshape(slab_rows, local_cols)
    weights = params.reshape(owned_rows, local_cols)
    own = lax.dynamic_slice_in_dim(grad, first_row, owned_rows, 0)
    old_rows = lax.dynamic_slice_in_dim(row_second.reshape(slab_rows, 1), first_row, owned_rows, 0)
    old_rows = jnp.broadcast_to(old_rows, (owned_rows, lanes))
    old_cols = col_second.reshape(1, local_cols)

    slots = []
    for slot in range((replicas - 1) * pieces):
        step, piece = divmod(slot, pieces)
        arrived = slots[slot - pieces] if step else ()
        tokens = slots[slot - in_flight] if slot >= in_flight and in_flight != pieces else ()
        owners = (replicas - 1 - step, step - (replicas - 1))
        right, left = make_partials(grad, arrived, tokens, owners, replicas, pieces, piece, piece_rows)
        to_right = [(i, i + 1) for i in range(step + 1)]
        to_left = [(replicas - 1 - i, replicas - 2 - i) for i in range(step + 1)]
        slots.append((lax.ppermute(right, "dp", to_right), lax.ppermute(left, "dp", to_left)))

    gradient = []
    new_row = []
    sums = None
    for piece in range(pieces):
        arrived = slots[len(slots) - pieces + piece]
        tokens = () if sums is None else (sums,)
        grad_piece, row_part, col_part = finish_piece(own, arrived, tokens, piece, piece_rows)
        row_parts = [row_part] + other_parts(row_part, "col")
        row_piece, sums = scale_piece(
            grad_piece, row_parts, old_rows, col_part, sums, hidden_width, piece, piece_rows
        )
        gradient.append(grad_piece)
        new_row.append(row_piece)
    sums = axis_sum(axis_sum(sums, "row"), "dp")
    new_col, update_part = column_factor(sums, old_cols, matrix_rows)
    updates = [update_part] + other_parts(update_part, "col")
    new_params = apply_update(
        weights, gradient, new_row, new_col, sums, updates, matrix_rows, hidden_width
    )
    new_row = jnp.concatenate([row[:, 0] for row in new_row])
    return (new_params.reshape(params.shape), new_row.reshape(1, 1, owned_rows), new_col)


def solution(mesh):
    return jax.shard_map(
        shards,
        mesh=mesh,
        in_specs=(
            P("dp", None, "row", None, "col"),
            P(None, "row", "dp", "col"),
            P(None, "row", None),
            P(None, "col"),
        ),
        out_specs=(P(None, "row", "dp", "col"), P(None, "row", "dp"), P(None, "col")),
        check_vma=False,
    )
```

```python
import jax
import jax.numpy as jnp
from jax import lax
from jax.experimental import pallas as pl
from jax.experimental.pallas import tpu as pltpu
from jax.sharding import PartitionSpec as P

beta_two = 1.0 - 8.0 ** (-0.8)
step_rate = 0.5
tiny_add = 1e-30
lanes = 128
ON_CHIP = pl.BlockSpec(memory_space=pltpu.VMEM)
IN_PLACE = pl.BlockSpec(memory_space=pltpu.HBM)
limits = pltpu.CompilerParams(vmem_limit_bytes=8 * 1024 * 1024)


def f32(*shape):
    return jax.ShapeDtypeStruct(shape, jnp.float32)


def cost(elements, flops, width):
    return pl.CostEstimate(flops=flops * elements, bytes_accessed=width * elements, transcendentals=0)


def axis_sum(values, axis):
    size = lax.axis_size(axis)
    hop = 1
    while hop < size:
        pairs = [(i, i ^ hop) for i in range(size)]
        values = values + lax.ppermute(values, axis, pairs)
        hop *= 2
    return values


def other_parts(values, axis):
    size = lax.axis_size(axis)
    return [lax.ppermute(values, axis, [(i, (i + k) % size) for i in range(size)]) for k in range(1, size)]


def pick(table):
    place = lax.axis_index("dp")
    value = jnp.int32(table[0])
    for k in range(1, len(table)):
        value = jnp.where(place == k, jnp.int32(table[k]), value)
    return value


def block_sum(grad, table, arrived, tokens, rows, fetch=False):
    cols = grad.shape[1]

    def body(grad_ref, *refs):
        start = pl.multiple_of(pick(table) * rows, rows)
        out_ref = refs[len(arrived) + len(tokens)]
        if fetch:
            own, sem = refs[-2:]
            copy = pltpu.make_async_copy(grad_ref.at[pl.ds(start, rows), :], own, sem)
            copy.start()
            copy.wait()
            values = own[...].astype(jnp.float32)
        else:
            values = grad_ref[pl.ds(start, rows), :].astype(jnp.float32)
        for ref in refs[: len(arrived)]:
            values = values + ref[...]
        out_ref[...] = values

    scratch = [pltpu.VMEM((rows, cols), grad.dtype), pltpu.SemaphoreType.DMA(())] if fetch else []
    if fetch:
        grad = pltpu.with_memory_space_constraint(grad, pltpu.HBM)
    return pl.pallas_call(
        body,
        out_shape=f32(rows, cols),
        in_specs=[IN_PLACE if fetch else ON_CHIP] + [ON_CHIP] * (len(arrived) + len(tokens)),
        out_specs=ON_CHIP,
        scratch_shapes=scratch,
        compiler_params=limits,
        cost_estimate=cost(rows * cols, 1, 10),
        name="block",
    )(grad, *arrived, *tokens)


def pass_on(values, tokens):
    def body(values_ref, *refs):
        refs[-1][...] = values_ref[...]

    return pl.pallas_call(
        body,
        out_shape=f32(*values.shape),
        in_specs=[ON_CHIP] * (1 + len(tokens)),
        out_specs=ON_CHIP,
        compiler_params=limits,
        cost_estimate=cost(values.size, 1, 8),
        name="pass",
    )(values, *tokens)


def finish_block(grad, table, arrived, rows):
    cols = grad.shape[1]

    def body(grad_ref, *refs):
        out_ref, row_ref, col_ref = refs[-3:]
        start = pl.multiple_of(pick(table) * rows, rows)
        for k in range(cols // lanes):
            at = pl.ds(k * lanes, lanes)
            values = grad_ref[pl.ds(start, rows), at].astype(jnp.float32)
            for ref in refs[: len(arrived)]:
                values = values + ref[:, at]
            out_ref[:, at] = values
            squares = values * values + tiny_add
            row_part = squares if k == 0 else row_part + squares
            col_ref[:, at] = jnp.sum(squares, axis=0, keepdims=True)
        row_ref[...] = row_part

    return pl.pallas_call(
        body,
        out_shape=(f32(rows, cols), f32(rows, lanes), f32(1, cols)),
        in_specs=[ON_CHIP] * (1 + len(arrived)),
        out_specs=(ON_CHIP,) * 3,
        compiler_params=limits,
        cost_estimate=cost(rows * cols, 6, 14),
        name="finish",
    )(grad, *arrived)


def diagonal(rows):
    row = lax.broadcasted_iota(jnp.int32, (rows, lanes), 0)
    return row == lax.broadcasted_iota(jnp.int32, (rows, lanes), 1)


def unpack_rows(sums, cols, count, rows):
    def body(sums_ref, *outs):
        for k, out in enumerate(outs):
            values = sums_ref[:, pl.ds(2 * cols + (k + 1) * lanes, lanes)]
            column = jnp.sum(jnp.where(diagonal(rows), values, 0.0), axis=1, keepdims=True)
            out[...] = jnp.broadcast_to(column, (rows, lanes))

    return pl.pallas_call(
        body,
        out_shape=(f32(rows, lanes),) * count,
        in_specs=[ON_CHIP],
        out_specs=(ON_CHIP,) * count,
        compiler_params=limits,
        cost_estimate=cost(rows * lanes, 2, 8),
        name="unpack",
    )(sums)


def scale_block(gradient, table, counted, row_parts, old_rows, col_part, held, carried, hidden_width):
    rows, cols = gradient.shape

    def body(grad_ref, col_ref, old_ref, *refs):
        row_out, sums_out = refs[-2:]
        total = refs[0][...]
        for ref in refs[1 : len(row_parts)]:
            total = total + ref[...]
        row_sum = jnp.sum(total, axis=1, keepdims=True)
        old = old_ref[pl.ds(pl.multiple_of(pick(table) * rows, rows), rows), :]
        row = beta_two * old + (1.0 - beta_two) * (row_sum / hidden_width)
        row_out[...] = row
        inverse = 1.0 / row
        before = refs[len(row_parts) : len(row_parts) + len(held)]
        counts = pick(counted) > 0

        def put(at, value):
            value = jnp.where(counts, value, 0.0)
            for ref in before:
                value = value + ref[:, at]
            sums_out[:, at] = value

        put(pl.ds(2 * cols, lanes), jnp.sum(row, axis=0, keepdims=True))
        for k in range(len(carried)):
            values = refs[len(row_parts) + len(held) + k][...]
            at = pl.ds(2 * cols + (k + 1) * lanes, lanes)
            sums_out[:, at] = jnp.sum(jnp.where(diagonal(rows), values, 0.0), axis=0, keepdims=True)
        for k in range(cols // lanes):
            at = pl.ds(k * lanes, lanes)
            values = grad_ref[:, at]
            put(at, col_ref[:, at])
            put(pl.ds(cols + k * lanes, lanes), jnp.sum(values * values * inverse, axis=0, keepdims=True))

    return pl.pallas_call(
        body,
        out_shape=(f32(rows, lanes), f32(1, 2 * cols + (1 + len(carried)) * lanes)),
        in_specs=[ON_CHIP] * (3 + len(row_parts) + len(held) + len(carried)),
        out_specs=(ON_CHIP, ON_CHIP),
        compiler_params=limits,
        cost_estimate=cost(rows * cols, 4, 4),
        name="scale",
    )(gradient, col_part, old_rows, *row_parts, *held, *carried)


def column_factor(sums, extra, old_cols, matrix_rows):
    cols = old_cols.shape[1]

    def body(sums_ref, old_ref, *refs):
        col_out, scale_out, update_out, mean_out = refs[-4:]
        weight = 1.0
        if extra:
            place = lax.axis_index("dp")
            ends = jnp.logical_or(place == 0, place == lax.axis_size("dp") - 1)
            weight = jnp.where(ends, 0.0, 1.0)

        def total(at):
            value = sums_ref[:, at]
            if extra:
                value = value * weight
            for ref in refs[: len(extra)]:
                value = value + ref[:, at]
            return value

        col = beta_two * old_ref[...] + (1.0 - beta_two) * (total(pl.ds(0, cols)) / matrix_rows)
        col_out[...] = col
        scale_out[...] = lax.rsqrt(col)
        ratio = total(pl.ds(cols, cols)) / col
        update = ratio[:, :lanes]
        for k in range(1, cols // lanes):
            update = update + ratio[:, k * lanes : (k + 1) * lanes]
        update_out[...] = update
        mean_out[...] = total(pl.ds(2 * cols, lanes)) / matrix_rows

    return pl.pallas_call(
        body,
        out_shape=(f32(1, cols), f32(1, cols), f32(1, lanes), f32(1, lanes)),
        in_specs=[ON_CHIP] * (2 + len(extra)),
        out_specs=(ON_CHIP,) * 4,
        compiler_params=limits,
        cost_estimate=cost(cols, 4, 12),
        name="columns",
    )(sums, old_cols, *extra)


def apply_update(weights, choices, part, held_out, col_scale, row_mean, updates, matrix_rows, hidden_width):
    pieces = len(choices[0][1])
    choices = [(places, gradient[part], new_row[part]) for places, gradient, new_row in choices]
    first = part.start
    count = len(choices[0][1])
    rows, cols = choices[0][1][0].shape
    arrays = [array for _, gradient, new_row in choices for array in (*gradient, *new_row)]

    def body(weights_ref, col_ref, mean_ref, *refs):
        update_refs = refs[len(arrays) : len(arrays) + len(updates)]
        out_ref, held, sems = refs[-3:]
        update_total = update_refs[0][...]
        for ref in update_refs[1:]:
            update_total = update_total + ref[...]
        update_total = jnp.sum(update_total, axis=1, keepdims=True)
        row_mean = mean_ref[:, :1]
        clip_ratio = jnp.sqrt(update_total * row_mean / (matrix_rows * hidden_width))
        factor = step_rate * jnp.sqrt(row_mean) / jnp.maximum(1.0, clip_ratio)
        col_factor = factor * col_ref[...]
        place = lax.axis_index("dp")

        def copy(k):
            here = held.at[pl.ds(k * rows, rows), :]
            return pltpu.make_async_copy(here, out_ref.at[pl.ds((first + k) * rows, rows), :], sems.at[k])

        for k in range(count):
            here = pl.ds(k * rows, rows)
            for c, (places, _, _) in enumerate(choices):
                grad_ref = refs[c * 2 * count + k]
                row_ref = refs[c * 2 * count + count + k]

                def write(k=k, grad_ref=grad_ref, row_ref=row_ref, here=here):
                    row_scale = lax.rsqrt(row_ref[:, :1])
                    mine = weights_ref[(first + k) * rows : (first + k + 1) * rows, :]
                    held[here, :] = mine - grad_ref[...] * row_scale * col_factor

                if len(choices) == 1:
                    write()
                else:
                    chosen = place == places[0]
                    for other in places[1:]:
                        chosen = jnp.logical_or(chosen, place == other)
                    pl.when(chosen)(write)
            copy(k).start()
        for k in range(count):
            copy(k).wait()

    return pl.pallas_call(
        body,
        out_shape=f32(rows * pieces, cols),
        in_specs=[ON_CHIP] * (3 + len(arrays) + len(updates)) + [IN_PLACE] * len(held_out),
        out_specs=IN_PLACE,
        scratch_shapes=[pltpu.VMEM((rows * count, cols), jnp.float32), pltpu.SemaphoreType.DMA((count,))],
        input_output_aliases={3 + len(arrays) + len(updates): 0} if held_out else {},
        compiler_params=limits,
        cost_estimate=cost(rows * count * cols, 4, 12),
        name="apply",
    )(weights, col_scale, row_mean, *arrays, *updates, *held_out)


def short_line(grad, old_rows, hidden_width, pieces, rows):
    last = 3
    late = range(pieces // 2, pieces)
    soon = range(pieces // 2)
    order = [(2, p) for p in late] + [(3, p) for p in range(pieces)] + [(2, p) for p in soon]
    order += [(1, p) for p in soon] + [(1, p) for p in late]
    swap = [(0, 1), (1, 0), (2, 3), (3, 2)]
    middle = [(1, 2), (2, 1)]
    outward = [(0, 1), (3, 2)]
    ends = [0, last]

    def right(m):
        shard, piece = order[min(max(m, 0), len(order) - 1)]
        return shard * pieces + piece

    def left(m):
        shard, piece = order[min(max(m, 0), len(order) - 1)]
        return (last - shard) * pieces + piece

    P, M = {}, {}
    finished, new_row = {}, {}
    sums = []

    def settle(slot, extra=()):
        table = [left(slot - 3), right(slot), left(slot), right(slot - 3)]
        counted = [int(slot <= 8), int(slot >= 8), int(slot >= 8), int(slot <= 8)]
        arrived = [P[slot]] + ([M[slot]] if slot >= 8 else [])
        gradient, row_part, col_part = finish_block(grad, table, arrived, rows)
        row_parts = [row_part] + other_parts(row_part, "col")
        finished[slot] = gradient
        carried = [new_row[3], new_row[4]] if slot == 8 else []
        new_row[slot], total = scale_block(
            gradient, table, counted, row_parts, old_rows, col_part, [*sums[-1:], *extra], carried, hidden_width
        )
        sums.append(total)

    for slot in range(10):
        if slot >= 2:
            operand = block_sum(grad, [0, right(slot - 2), left(slot - 2), 0], [P[slot - 2]], [], rows)
            M[slot] = lax.ppermute(operand, "dp", middle)
        table = [right(slot), left(slot - 3), right(slot - 3), left(slot)]
        arrived = [M[slot - 1]] if slot >= 3 else []
        tokens = [P[0]] if slot == 2 else []
        operand = block_sum(grad, table, arrived, tokens, rows, fetch=slot < 2)
        P[slot] = lax.ppermute(operand, "dp", swap)
        if 3 <= slot <= 8:
            settle(slot)
    early = lax.ppermute(sums[-1], "dp", outward)
    late_rows = unpack_rows(early, grad.shape[1], 2, rows)
    operand = pass_on(finished[3], [sums[-1]])
    P[10] = lax.ppermute(operand, "dp", outward)
    P[11] = lax.ppermute(pass_on(finished[4], [operand]), "dp", outward)
    settle(9, [early])
    total = axis_sum(sums[-1], "row")
    total = total + lax.ppermute(total, "dp", middle)
    extra = [lax.ppermute(total, "dp", [(1, 0), (2, 3)])]
    outer = ([finished[k] for k in range(5, 9)], [new_row[k] for k in range(5, 9)])
    inner = (
        [finished[8], finished[9], P[10], P[11]],
        [new_row[8], new_row[9], *late_rows],
    )
    return total, extra, [(ends, *outer), ([1, 2], *inner)]


def long_line(grad, old_rows, hidden_width, pieces, rows):
    replicas = lax.axis_size("dp")
    to_right = [(i, i + 1) for i in range(replicas - 1)]
    to_left = [(i + 1, i) for i in range(replicas - 1)]
    rights, lefts = {}, {}
    for slot in range((replicas - 1) * pieces):
        step, piece = divmod(slot, pieces)
        right_table = [min(replicas - 1 - step + z, replicas - 1) * pieces + piece for z in range(replicas)]
        left_table = [max(step - (replicas - 1) + z, 0) * pieces + piece for z in range(replicas)]
        before = slot - pieces
        right = block_sum(grad, right_table, [rights[before]] if step else [], [], rows)
        left = block_sum(grad, left_table, [lefts[before]] if step else [], [], rows)
        rights[slot] = lax.ppermute(right, "dp", to_right[: step + 1])
        lefts[slot] = lax.ppermute(left, "dp", to_left[replicas - 2 - step :])
    gradient, new_row, held = [], [], []
    for piece in range(pieces):
        slot = (replicas - 2) * pieces + piece
        table = [z * pieces + piece for z in range(replicas)]
        grad_piece, row_part, col_part = finish_block(grad, table, [rights[slot], lefts[slot]], rows)
        row_parts = [row_part] + other_parts(row_part, "col")
        row_piece, sums = scale_block(
            grad_piece, table, [1] * replicas, row_parts, old_rows, col_part, held, [], hidden_width
        )
        held = [sums]
        gradient.append(grad_piece)
        new_row.append(row_piece)
    total = axis_sum(axis_sum(sums, "row"), "dp")
    return total, [], [(list(range(replicas)), gradient, new_row)]


def shards(grad_parts, params, row_second, col_second):
    owned_rows = params.shape[2]
    local_cols = params.shape[3]
    slab_rows = row_second.shape[2]
    hidden_width = local_cols * lax.axis_size("col")
    matrix_rows = slab_rows * lax.axis_size("row")
    replicas = lax.axis_size("dp")
    pieces = max(1, min(4, owned_rows // 16))
    rows = owned_rows // pieces
    grad = grad_parts.reshape(slab_rows, local_cols)
    weights = params.reshape(owned_rows, local_cols)
    old_rows = jnp.broadcast_to(row_second.reshape(slab_rows, 1), (slab_rows, lanes))
    old_cols = col_second.reshape(1, local_cols)
    line = short_line if replicas == 4 and pieces == 4 else long_line
    total, extra, choices = line(grad, old_rows, hidden_width, pieces, rows)
    new_col, col_scale, update_part, row_mean = column_factor(total, extra, old_cols, matrix_rows)
    updates = [update_part] + other_parts(update_part, "col")
    new_params = []
    for part in (slice(0, pieces - 1), slice(pieces - 1, pieces)) if pieces > 1 else (slice(0, 1),):
        new_params = [
            apply_update(
                weights, choices, part, new_params, col_scale, row_mean, updates, matrix_rows, hidden_width
            )
        ]
    new_params = new_params[0]
    new_row = [jnp.concatenate([row[:, 0] for row in rows_here]) for _, _, rows_here in choices]
    place = lax.axis_index("dp")
    if len(choices) > 1:
        inner = jnp.logical_and(place > 0, place < replicas - 1)
        new_row = [jnp.where(inner, new_row[1], new_row[0])]
    return (new_params.reshape(params.shape), new_row[0].reshape(1, 1, owned_rows), new_col)


def solution(mesh):
    return jax.shard_map(
        shards,
        mesh=mesh,
        in_specs=(
            P("dp", None, "row", None, "col"),
            P(None, "row", "dp", "col"),
            P(None, "row", None),
            P(None, "col"),
        ),
        out_specs=(P(None, "row", "dp", "col"), P(None, "row", "dp"), P(None, "col")),
        check_vma=False,
    )
```

```python
import jax
import jax.numpy as jnp
from jax import lax
from jax.experimental import pallas as pl
from jax.experimental.pallas import tpu as pltpu
from jax.sharding import PartitionSpec as P

beta_two = 1.0 - 8.0 ** (-0.8)
step_rate = 0.5
tiny_add = 1e-30
lanes = 128
ON_CHIP = pl.BlockSpec(memory_space=pltpu.VMEM)
IN_PLACE = pl.BlockSpec(memory_space=pltpu.HBM)
limits = pltpu.CompilerParams(vmem_limit_bytes=8 * 1024 * 1024)


def f32(*shape):
    return jax.ShapeDtypeStruct(shape, jnp.float32)


def cost(elements, flops, width):
    return pl.CostEstimate(flops=flops * elements, bytes_accessed=width * elements, transcendentals=0)


def axis_sum(values, axis):
    size = lax.axis_size(axis)
    hop = 1
    while hop < size:
        pairs = [(i, i ^ hop) for i in range(size)]
        values = values + lax.ppermute(values, axis, pairs)
        hop *= 2
    return values


def other_parts(values, axis):
    size = lax.axis_size(axis)
    return [lax.ppermute(values, axis, [(i, (i + k) % size) for i in range(size)]) for k in range(1, size)]


def pick(table):
    place = lax.axis_index("dp")
    value = jnp.int32(table[0])
    for k in range(1, len(table)):
        value = jnp.where(place == k, jnp.int32(table[k]), value)
    return value


def block_sum(grad, table, arrived, tokens, rows):
    cols = grad.shape[1]

    def body(grad_ref, *refs):
        start = pl.multiple_of(pick(table) * rows, rows)
        values = grad_ref[pl.ds(start, rows), :].astype(jnp.float32)
        for ref in refs[: len(arrived)]:
            values = values + ref[...]
        refs[-1][...] = values

    return pl.pallas_call(
        body,
        out_shape=f32(rows, cols),
        in_specs=[ON_CHIP] * (1 + len(arrived) + len(tokens)),
        out_specs=ON_CHIP,
        compiler_params=limits,
        cost_estimate=cost(rows * cols, 1, 10),
        name="block",
    )(grad, *arrived, *tokens)


def fetch_block(grad, table, places, rows):
    cols = grad.shape[1]
    chunk = min(rows, 8)

    def body(grad_ref, out_ref, held, sems):
        wanted = pick(places) > 0
        start = pick(table) * rows

        def copy(k):
            at = pl.ds(pl.multiple_of(start + k * chunk, chunk), chunk)
            return pltpu.make_async_copy(grad_ref.at[at, :], held.at[pl.ds(k * chunk, chunk), :], sems.at[k])

        @pl.when(wanted)
        def _():
            for k in range(rows // chunk):
                copy(k).start()
            for k in range(rows // chunk):
                at = pl.ds(k * chunk, chunk)
                copy(k).wait()
                out_ref[at, :] = held[at, :].astype(jnp.float32)

        @pl.when(jnp.logical_not(wanted))
        def _():
            out_ref[...] = jnp.zeros((rows, cols), jnp.float32)

    return pl.pallas_call(
        body,
        out_shape=f32(rows, cols),
        in_specs=[IN_PLACE],
        out_specs=ON_CHIP,
        scratch_shapes=[pltpu.VMEM((rows, cols), grad.dtype), pltpu.SemaphoreType.DMA((rows // chunk,))],
        compiler_params=limits,
        cost_estimate=cost(rows * cols, 1, 6),
        name="fetch",
    )(pltpu.with_memory_space_constraint(grad, pltpu.HBM))


def pass_on(values, tokens):
    def body(values_ref, *refs):
        refs[-1][...] = values_ref[...]

    return pl.pallas_call(
        body,
        out_shape=f32(*values.shape),
        in_specs=[ON_CHIP] * (1 + len(tokens)),
        out_specs=ON_CHIP,
        compiler_params=limits,
        cost_estimate=cost(values.size, 1, 8),
        name="pass",
    )(values, *tokens)


def finish_block(grad, table, arrived, rows):
    cols = arrived[0].shape[1]
    from_grad = [] if grad is None else [grad]

    def body(*refs):
        out_ref, row_ref, col_ref = refs[-3:]
        start = pl.multiple_of(pick(table) * rows, rows)
        sources = refs[len(from_grad) : len(from_grad) + len(arrived)]
        for k in range(cols // lanes):
            at = pl.ds(k * lanes, lanes)
            values = sources[0][:, at]
            for ref in sources[1:]:
                values = values + ref[:, at]
            if from_grad:
                values = values + refs[0][pl.ds(start, rows), at].astype(jnp.float32)
            out_ref[:, at] = values
            squares = values * values + tiny_add
            row_part = squares if k == 0 else row_part + squares
            col_ref[:, at] = jnp.sum(squares, axis=0, keepdims=True)
        row_ref[...] = row_part

    return pl.pallas_call(
        body,
        out_shape=(f32(rows, cols), f32(rows, lanes), f32(1, cols)),
        in_specs=[ON_CHIP] * (len(from_grad) + len(arrived)),
        out_specs=(ON_CHIP,) * 3,
        compiler_params=limits,
        cost_estimate=cost(rows * cols, 6, 14),
        name="finish",
    )(*from_grad, *arrived)


def diagonal(rows):
    row = lax.broadcasted_iota(jnp.int32, (rows, lanes), 0)
    return row == lax.broadcasted_iota(jnp.int32, (rows, lanes), 1)


def unpack_rows(sums, cols, count, rows):
    def body(sums_ref, *outs):
        for k, out in enumerate(outs):
            values = sums_ref[:, pl.ds(2 * cols + (k + 1) * lanes, lanes)]
            column = jnp.sum(jnp.where(diagonal(rows), values, 0.0), axis=1, keepdims=True)
            out[...] = jnp.broadcast_to(column, (rows, lanes))

    return pl.pallas_call(
        body,
        out_shape=(f32(rows, lanes),) * count,
        in_specs=[ON_CHIP],
        out_specs=(ON_CHIP,) * count,
        compiler_params=limits,
        cost_estimate=cost(rows * lanes, 2, 8),
        name="unpack",
    )(sums)


def scale_block(gradient, table, counted, row_parts, old_rows, col_part, held, carried, hidden_width):
    rows, cols = gradient.shape

    def body(grad_ref, col_ref, old_ref, *refs):
        row_out, sums_out = refs[-2:]
        total = refs[0][...]
        for ref in refs[1 : len(row_parts)]:
            total = total + ref[...]
        row_sum = jnp.sum(total, axis=1, keepdims=True)
        old = old_ref[pl.ds(pl.multiple_of(pick(table) * rows, rows), rows), :]
        row = beta_two * old + (1.0 - beta_two) * (row_sum / hidden_width)
        row_out[...] = row
        inverse = 1.0 / row
        before = refs[len(row_parts) : len(row_parts) + len(held)]
        counts = pick(counted) > 0

        def put(at, value):
            value = jnp.where(counts, value, 0.0)
            for ref in before:
                value = value + ref[:, at]
            sums_out[:, at] = value

        put(pl.ds(2 * cols, lanes), jnp.sum(row, axis=0, keepdims=True))
        for k in range(len(carried)):
            values = refs[len(row_parts) + len(held) + k][...]
            at = pl.ds(2 * cols + (k + 1) * lanes, lanes)
            sums_out[:, at] = jnp.sum(jnp.where(diagonal(rows), values, 0.0), axis=0, keepdims=True)
        for k in range(cols // lanes):
            at = pl.ds(k * lanes, lanes)
            values = grad_ref[:, at]
            put(at, col_ref[:, at])
            put(pl.ds(cols + k * lanes, lanes), jnp.sum(values * values * inverse, axis=0, keepdims=True))

    return pl.pallas_call(
        body,
        out_shape=(f32(rows, lanes), f32(1, 2 * cols + (1 + len(carried)) * lanes)),
        in_specs=[ON_CHIP] * (3 + len(row_parts) + len(held) + len(carried)),
        out_specs=(ON_CHIP, ON_CHIP),
        compiler_params=limits,
        cost_estimate=cost(rows * cols, 4, 4),
        name="scale",
    )(gradient, col_part, old_rows, *row_parts, *held, *carried)


def column_factor(sums, extra, old_cols, matrix_rows):
    cols = old_cols.shape[1]

    def body(sums_ref, old_ref, *refs):
        col_out, scale_out, update_out, mean_out = refs[-4:]
        weight = 1.0
        if extra:
            place = lax.axis_index("dp")
            ends = jnp.logical_or(place == 0, place == lax.axis_size("dp") - 1)
            weight = jnp.where(ends, 0.0, 1.0)

        def total(at):
            value = sums_ref[:, at]
            if extra:
                value = value * weight
            for ref in refs[: len(extra)]:
                value = value + ref[:, at]
            return value

        col = beta_two * old_ref[...] + (1.0 - beta_two) * (total(pl.ds(0, cols)) / matrix_rows)
        col_out[...] = col
        scale_out[...] = lax.rsqrt(col)
        ratio = total(pl.ds(cols, cols)) / col
        update = ratio[:, :lanes]
        for k in range(1, cols // lanes):
            update = update + ratio[:, k * lanes : (k + 1) * lanes]
        update_out[...] = update
        mean_out[...] = total(pl.ds(2 * cols, lanes)) / matrix_rows

    return pl.pallas_call(
        body,
        out_shape=(f32(1, cols), f32(1, cols), f32(1, lanes), f32(1, lanes)),
        in_specs=[ON_CHIP] * (2 + len(extra)),
        out_specs=(ON_CHIP,) * 4,
        compiler_params=limits,
        cost_estimate=cost(cols, 4, 12),
        name="columns",
    )(sums, old_cols, *extra)


def select_run(choices, action):
    place = lax.axis_index("dp")
    for c, (places, _, _) in enumerate(choices):
        if len(choices) == 1:
            action(c)
        else:
            chosen = place == places[0]
            for other in places[1:]:
                chosen = jnp.logical_or(chosen, place == other)
            pl.when(chosen)(lambda c=c: action(c))


def apply_first(weights, choices, col_scale, row_mean, updates, matrix_rows, hidden_width):
    pieces = len(choices[0][1])
    count = pieces - 1
    rows, cols = choices[0][1][0].shape
    arrays = [array for _, gradient, new_row in choices for array in (*gradient[:count], *new_row)]
    each = count + pieces

    def body(weights_ref, col_ref, mean_ref, *refs):
        update_refs = refs[len(arrays) : len(arrays) + len(updates)]
        out_ref, factor_ref, scale_ref, held, sems = refs[-5:]
        update_total = update_refs[0][...]
        for ref in update_refs[1:]:
            update_total = update_total + ref[...]
        update_total = jnp.sum(update_total, axis=1, keepdims=True)
        row_mean = mean_ref[:, :1]
        clip_ratio = jnp.sqrt(update_total * row_mean / (matrix_rows * hidden_width))
        factor = step_rate * jnp.sqrt(row_mean) / jnp.maximum(1.0, clip_ratio)
        col_factor = factor * col_ref[...]
        factor_ref[...] = col_factor

        def copy(k):
            here = pl.ds(k * rows, rows)
            return pltpu.make_async_copy(held.at[here, :], out_ref.at[here, :], sems.at[k])

        for k in range(count):

            def write(c, k=k):
                here = pl.ds(k * rows, rows)
                row_scale = lax.rsqrt(refs[c * each + count + k][:, :1])
                held[here, :] = weights_ref[here, :] - refs[c * each + k][...] * row_scale * col_factor

            select_run(choices, write)
            copy(k).start()

        def last_scale(c):
            scale_ref[...] = lax.rsqrt(refs[c * each + count + pieces - 1][...])

        select_run(choices, last_scale)
        for k in range(count):
            copy(k).wait()

    return pl.pallas_call(
        body,
        out_shape=(f32(rows * pieces, cols), f32(1, cols), f32(rows, lanes)),
        in_specs=[ON_CHIP] * (3 + len(arrays) + len(updates)),
        out_specs=(IN_PLACE, ON_CHIP, ON_CHIP),
        scratch_shapes=[pltpu.VMEM((rows * count, cols), jnp.float32), pltpu.SemaphoreType.DMA((count,))],
        compiler_params=limits,
        cost_estimate=cost(rows * count * cols, 4, 12),
        name="apply",
    )(weights, col_scale, row_mean, *arrays, *updates)


def apply_last(weights, choices, begun, col_factor, row_scale):
    pieces = len(choices[0][1])
    rows, cols = choices[0][1][0].shape
    chunk = min(rows, 8)
    first = (pieces - 1) * rows
    arrays = [gradient[-1] for _, gradient, _ in choices]

    def body(weights_ref, factor_ref, scale_ref, *refs):
        out_ref, held, sems = refs[-3:]

        def copy(k):
            here = held.at[pl.ds(k * chunk, chunk), :]
            return pltpu.make_async_copy(here, out_ref.at[pl.ds(first + k * chunk, chunk), :], sems.at[k])

        def write(c):
            for k in range(rows // chunk):
                here = pl.ds(k * chunk, chunk)
                step = refs[c][here, :] * scale_ref[here, :1] * factor_ref[...]
                held[here, :] = weights_ref[first + k * chunk : first + (k + 1) * chunk, :] - step
                copy(k).start()

        select_run(choices, write)
        for k in range(rows // chunk):
            copy(k).wait()

    return pl.pallas_call(
        body,
        out_shape=f32(rows * pieces, cols),
        in_specs=[ON_CHIP] * (3 + len(arrays)) + [IN_PLACE],
        out_specs=IN_PLACE,
        scratch_shapes=[pltpu.VMEM((rows, cols), jnp.float32), pltpu.SemaphoreType.DMA((rows // chunk,))],
        input_output_aliases={3 + len(arrays): 0},
        compiler_params=limits,
        cost_estimate=cost(rows * cols, 3, 12),
        name="last",
    )(weights, col_factor, row_scale, *arrays, begun)


def row_line(choices):
    count = len(choices[0][2])
    rows = choices[0][2][0].shape[0]
    arrays = [array for _, _, new_row in choices for array in new_row]

    def body(*refs):
        place = lax.axis_index("dp")
        row = lax.broadcasted_iota(jnp.int32, (rows, lanes), 0)
        lane = lax.broadcasted_iota(jnp.int32, (rows, lanes), 1)
        line = jnp.zeros((1, lanes), jnp.float32)
        for piece in range(count):
            values = refs[piece][...]
            for c, (places, _, _) in enumerate(choices[1:], 1):
                for other in places:
                    values = jnp.where(place == other, refs[c * count + piece][...], values)
            at = lane == row + piece * rows
            line = line + jnp.sum(jnp.where(at, values, 0.0), axis=0, keepdims=True)
        refs[-1][...] = line

    return pl.pallas_call(
        body,
        out_shape=f32(1, lanes),
        in_specs=[ON_CHIP] * len(arrays),
        out_specs=ON_CHIP,
        compiler_params=limits,
        cost_estimate=cost(rows * count * lanes, 2, 4),
        name="rows",
    )(*arrays)


def short_line(grad, old_rows, hidden_width, pieces, rows):
    last = 3
    late = range(pieces // 2, pieces)
    soon = range(pieces // 2)
    order = [(2, p) for p in late] + [(3, p) for p in range(pieces)] + [(2, p) for p in soon]
    order += [(1, p) for p in soon] + [(1, p) for p in late]
    swap = [(0, 1), (1, 0), (2, 3), (3, 2)]
    middle = [(1, 2), (2, 1)]
    outward = [(0, 1), (3, 2)]
    ends = [0, last]

    def right(m):
        shard, piece = order[min(max(m, 0), len(order) - 1)]
        return shard * pieces + piece

    def left(m):
        shard, piece = order[min(max(m, 0), len(order) - 1)]
        return (last - shard) * pieces + piece

    P, M, fetched = {}, {}, {}
    finished, new_row = {}, {}
    sums = []

    def own_table(slot):
        return [left(slot - 3), right(slot), left(slot), right(slot - 3)]

    def settle(slot, extra=()):
        table = own_table(slot)
        counted = [int(slot <= 8), int(slot >= 8), int(slot >= 8), int(slot <= 8)]
        arrived = [P[slot], M[slot], fetched[slot]] if slot >= 8 else [P[slot]]
        gradient, row_part, col_part = finish_block(None if slot >= 8 else grad, table, arrived, rows)
        row_parts = [row_part] + other_parts(row_part, "col")
        finished[slot] = gradient
        carried = [new_row[3], new_row[4]] if slot == 8 else []
        new_row[slot], total = scale_block(
            gradient, table, counted, row_parts, old_rows, col_part, [*sums[-1:], *extra], carried, hidden_width
        )
        sums.append(total)

    for slot in range(10):
        if slot >= 2:
            operand = block_sum(grad, [0, right(slot - 2), left(slot - 2), 0], [P[slot - 2]], [], rows)
            M[slot] = lax.ppermute(operand, "dp", middle)
        table = [right(slot), left(slot - 3), right(slot - 3), left(slot)]
        arrived = [M[slot - 1]] if slot >= 3 else []
        if slot < 2:
            operand = fetch_block(grad, table, [1, 0, 0, 1], rows)
        else:
            tokens = [P[0]] if slot == 2 else list(fetched.values()) if slot == 7 else []
            operand = block_sum(grad, table, arrived, tokens, rows)
        P[slot] = lax.ppermute(operand, "dp", swap)
        if slot == 5:
            fetched |= {k: fetch_block(grad, own_table(k), [1, 1, 1, 1], rows) for k in (8, 9)}
        if 3 <= slot <= 8:
            settle(slot)
    early = lax.ppermute(sums[-1], "dp", outward)
    late_rows = unpack_rows(early, grad.shape[1], 2, rows)
    operand = pass_on(finished[3], [sums[-1]])
    P[10] = lax.ppermute(operand, "dp", outward)
    P[11] = lax.ppermute(pass_on(finished[4], [operand, early]), "dp", outward)
    settle(9, [early])
    total = axis_sum(sums[-1], "row")
    total = total + lax.ppermute(total, "dp", middle)
    extra = [lax.ppermute(total, "dp", [(1, 0), (2, 3)])]
    outer = ([finished[k] for k in range(5, 9)], [new_row[k] for k in range(5, 9)])
    inner = (
        [finished[8], finished[9], P[10], P[11]],
        [new_row[8], new_row[9], *late_rows],
    )
    return total, extra, [(ends, *outer), ([1, 2], *inner)]


def long_line(grad, old_rows, hidden_width, pieces, rows):
    replicas = lax.axis_size("dp")
    to_right = [(i, i + 1) for i in range(replicas - 1)]
    to_left = [(i + 1, i) for i in range(replicas - 1)]
    rights, lefts = {}, {}
    for slot in range((replicas - 1) * pieces):
        step, piece = divmod(slot, pieces)
        right_table = [min(replicas - 1 - step + z, replicas - 1) * pieces + piece for z in range(replicas)]
        left_table = [max(step - (replicas - 1) + z, 0) * pieces + piece for z in range(replicas)]
        before = slot - pieces
        right = block_sum(grad, right_table, [rights[before]] if step else [], [], rows)
        left = block_sum(grad, left_table, [lefts[before]] if step else [], [], rows)
        rights[slot] = lax.ppermute(right, "dp", to_right[: step + 1])
        lefts[slot] = lax.ppermute(left, "dp", to_left[replicas - 2 - step :])
    gradient, new_row, held = [], [], []
    for piece in range(pieces):
        slot = (replicas - 2) * pieces + piece
        table = [z * pieces + piece for z in range(replicas)]
        grad_piece, row_part, col_part = finish_block(grad, table, [rights[slot], lefts[slot]], rows)
        row_parts = [row_part] + other_parts(row_part, "col")
        row_piece, sums = scale_block(
            grad_piece, table, [1] * replicas, row_parts, old_rows, col_part, held, [], hidden_width
        )
        held = [sums]
        gradient.append(grad_piece)
        new_row.append(row_piece)
    total = axis_sum(axis_sum(sums, "row"), "dp")
    return total, [], [(list(range(replicas)), gradient, new_row)]


def shards(grad_parts, params, row_second, col_second):
    owned_rows = params.shape[2]
    local_cols = params.shape[3]
    slab_rows = row_second.shape[2]
    hidden_width = local_cols * lax.axis_size("col")
    matrix_rows = slab_rows * lax.axis_size("row")
    replicas = lax.axis_size("dp")
    pieces = 4 if owned_rows >= 64 else 2
    rows = owned_rows // pieces
    grad = grad_parts.reshape(slab_rows, local_cols)
    weights = params.reshape(owned_rows, local_cols)
    old_rows = jnp.broadcast_to(row_second.reshape(slab_rows, 1), (slab_rows, lanes))
    old_cols = col_second.reshape(1, local_cols)
    line = short_line if replicas == 4 and pieces == 4 else long_line
    total, extra, choices = line(grad, old_rows, hidden_width, pieces, rows)
    new_col, col_scale, update_part, row_mean = column_factor(total, extra, old_cols, matrix_rows)
    updates = [update_part] + other_parts(update_part, "col")
    begun, col_factor, row_scale = apply_first(
        weights, choices, col_scale, row_mean, updates, matrix_rows, hidden_width
    )
    new_params = apply_last(weights, choices, begun, col_factor, row_scale)
    new_row = row_line(choices)[:, :owned_rows]
    return (new_params.reshape(params.shape), new_row.reshape(1, 1, owned_rows), new_col)


def solution(mesh):
    return jax.shard_map(
        shards,
        mesh=mesh,
        in_specs=(
            P("dp", None, "row", None, "col"),
            P(None, "row", "dp", "col"),
            P(None, "row", None),
            P(None, "col"),
        ),
        out_specs=(P(None, "row", "dp", "col"), P(None, "row", "dp"), P(None, "col")),
        check_vma=False,
    )
```

```python
import jax
import jax.numpy as jnp
from jax import lax
from jax.experimental import pallas as pl
from jax.experimental.pallas import tpu as pltpu
from jax.sharding import PartitionSpec as P

beta_two = 1.0 - 8.0 ** (-0.8)
step_rate = 0.5
tiny_add = 1e-30
lanes = 128
ON_CHIP = pl.BlockSpec(memory_space=pltpu.VMEM)
IN_PLACE = pl.BlockSpec(memory_space=pltpu.HBM)
limits = pltpu.CompilerParams(vmem_limit_bytes=8 * 1024 * 1024)


def f32(*shape):
    return jax.ShapeDtypeStruct(shape, jnp.float32)


def cost(elements, flops, width):
    return pl.CostEstimate(flops=flops * elements, bytes_accessed=width * elements, transcendentals=0)


def axis_sum(values, axis):
    size = lax.axis_size(axis)
    hop = 1
    while hop < size:
        pairs = [(i, i ^ hop) for i in range(size)]
        values = values + lax.ppermute(values, axis, pairs)
        hop *= 2
    return values


def other_parts(values, axis):
    size = lax.axis_size(axis)
    return [lax.ppermute(values, axis, [(i, (i + k) % size) for i in range(size)]) for k in range(1, size)]


def pick(table):
    place = lax.axis_index("dp")
    value = jnp.int32(table[0])
    for k in range(1, len(table)):
        value = jnp.where(place == k, jnp.int32(table[k]), value)
    return value


def block_sum(grad, table, arrived, tokens, rows):
    cols = grad.shape[1]

    def body(grad_ref, *refs):
        start = pl.multiple_of(pick(table) * rows, rows)
        values = grad_ref[pl.ds(start, rows), :].astype(jnp.float32)
        for ref in refs[: len(arrived)]:
            values = values + ref[...]
        refs[-1][...] = values

    return pl.pallas_call(
        body,
        out_shape=f32(rows, cols),
        in_specs=[ON_CHIP] * (1 + len(arrived) + len(tokens)),
        out_specs=ON_CHIP,
        compiler_params=limits,
        cost_estimate=cost(rows * cols, 1, 10),
        name="block",
    )(grad, *arrived, *tokens)


def stage_gradient(grad, tokens):
    def body(grad_ref, *refs):
        out_ref, sem = refs[-2:]
        copy = pltpu.make_async_copy(grad_ref, out_ref, sem)
        copy.start()
        copy.wait()

    return pl.pallas_call(
        body,
        out_shape=jax.ShapeDtypeStruct(grad.shape, grad.dtype),
        in_specs=[IN_PLACE] + [ON_CHIP] * len(tokens),
        out_specs=ON_CHIP,
        scratch_shapes=[pltpu.SemaphoreType.DMA(())],
        compiler_params=limits,
        cost_estimate=cost(grad.size, 0, 2),
        name="stage",
    )(pltpu.with_memory_space_constraint(grad, pltpu.HBM), *tokens)


def fetch_block(grad, table, places, rows):
    cols = grad.shape[1]
    chunk = min(rows, 8)

    def body(grad_ref, out_ref, held, sems):
        wanted = pick(places) > 0
        start = pick(table) * rows

        def copy(k):
            at = pl.ds(pl.multiple_of(start + k * chunk, chunk), chunk)
            return pltpu.make_async_copy(grad_ref.at[at, :], held.at[pl.ds(k * chunk, chunk), :], sems.at[k])

        @pl.when(wanted)
        def _():
            for k in range(rows // chunk):
                copy(k).start()
            for k in range(rows // chunk):
                at = pl.ds(k * chunk, chunk)
                copy(k).wait()
                out_ref[at, :] = held[at, :].astype(jnp.float32)

        @pl.when(jnp.logical_not(wanted))
        def _():
            out_ref[...] = jnp.zeros((rows, cols), jnp.float32)

    return pl.pallas_call(
        body,
        out_shape=f32(rows, cols),
        in_specs=[IN_PLACE],
        out_specs=ON_CHIP,
        scratch_shapes=[pltpu.VMEM((rows, cols), grad.dtype), pltpu.SemaphoreType.DMA((rows // chunk,))],
        compiler_params=limits,
        cost_estimate=cost(rows * cols, 1, 6),
        name="fetch",
    )(pltpu.with_memory_space_constraint(grad, pltpu.HBM))


def pass_on(values, tokens):
    def body(values_ref, *refs):
        refs[-1][...] = values_ref[...]

    return pl.pallas_call(
        body,
        out_shape=f32(*values.shape),
        in_specs=[ON_CHIP] * (1 + len(tokens)),
        out_specs=ON_CHIP,
        compiler_params=limits,
        cost_estimate=cost(values.size, 1, 8),
        name="pass",
    )(values, *tokens)


def finish_block(grad, table, arrived, rows):
    cols = arrived[0].shape[1]

    def body(grad_ref, *refs):
        out_ref, row_ref, col_ref = refs[-3:]
        start = pl.multiple_of(pick(table) * rows, rows)
        for k in range(cols // lanes):
            at = pl.ds(k * lanes, lanes)
            values = grad_ref[pl.ds(start, rows), at].astype(jnp.float32)
            for ref in refs[: len(arrived)]:
                values = values + ref[:, at]
            out_ref[:, at] = values
            squares = values * values + tiny_add
            row_part = squares if k == 0 else row_part + squares
            col_ref[:, at] = jnp.sum(squares, axis=0, keepdims=True)
        row_ref[...] = row_part

    return pl.pallas_call(
        body,
        out_shape=(f32(rows, cols), f32(rows, lanes), f32(1, cols)),
        in_specs=[ON_CHIP] * (1 + len(arrived)),
        out_specs=(ON_CHIP,) * 3,
        compiler_params=limits,
        cost_estimate=cost(rows * cols, 6, 14),
        name="finish",
    )(grad, *arrived)


def diagonal(rows):
    row = lax.broadcasted_iota(jnp.int32, (rows, lanes), 0)
    return row == lax.broadcasted_iota(jnp.int32, (rows, lanes), 1)


def unpack_rows(sums, cols, count, rows):
    def body(sums_ref, *outs):
        for k, out in enumerate(outs):
            values = sums_ref[:, pl.ds(2 * cols + (k + 1) * lanes, lanes)]
            column = jnp.sum(jnp.where(diagonal(rows), values, 0.0), axis=1, keepdims=True)
            out[...] = jnp.broadcast_to(column, (rows, lanes))

    return pl.pallas_call(
        body,
        out_shape=(f32(rows, lanes),) * count,
        in_specs=[ON_CHIP],
        out_specs=(ON_CHIP,) * count,
        compiler_params=limits,
        cost_estimate=cost(rows * lanes, 2, 8),
        name="unpack",
    )(sums)


def scale_block(gradient, table, counted, row_parts, old_rows, col_part, held, carried, hidden_width):
    rows, cols = gradient.shape

    def body(grad_ref, col_ref, old_ref, *refs):
        row_out, sums_out = refs[-2:]
        total = refs[0][...]
        for ref in refs[1 : len(row_parts)]:
            total = total + ref[...]
        row_sum = jnp.sum(total, axis=1, keepdims=True)
        old = old_ref[pl.ds(pl.multiple_of(pick(table) * rows, rows), rows), :]
        row = beta_two * old + (1.0 - beta_two) * (row_sum / hidden_width)
        row_out[...] = row
        inverse = 1.0 / row
        before = refs[len(row_parts) : len(row_parts) + len(held)]
        counts = pick(counted) > 0

        def put(at, value):
            value = jnp.where(counts, value, 0.0)
            for ref in before:
                value = value + ref[:, at]
            sums_out[:, at] = value

        put(pl.ds(2 * cols, lanes), jnp.sum(row, axis=0, keepdims=True))
        for k in range(len(carried)):
            values = refs[len(row_parts) + len(held) + k][...]
            at = pl.ds(2 * cols + (k + 1) * lanes, lanes)
            sums_out[:, at] = jnp.sum(jnp.where(diagonal(rows), values, 0.0), axis=0, keepdims=True)
        for k in range(cols // lanes):
            at = pl.ds(k * lanes, lanes)
            values = grad_ref[:, at]
            put(at, col_ref[:, at])
            put(pl.ds(cols + k * lanes, lanes), jnp.sum(values * values * inverse, axis=0, keepdims=True))

    return pl.pallas_call(
        body,
        out_shape=(f32(rows, lanes), f32(1, 2 * cols + (1 + len(carried)) * lanes)),
        in_specs=[ON_CHIP] * (3 + len(row_parts) + len(held) + len(carried)),
        out_specs=(ON_CHIP, ON_CHIP),
        compiler_params=limits,
        cost_estimate=cost(rows * cols, 4, 4),
        name="scale",
    )(gradient, col_part, old_rows, *row_parts, *held, *carried)


def column_factor(sums, extra, old_cols, matrix_rows):
    cols = old_cols.shape[1]

    def body(sums_ref, old_ref, *refs):
        col_out, scale_out, update_out, mean_out = refs[-4:]
        weight = 1.0
        if extra:
            place = lax.axis_index("dp")
            ends = jnp.logical_or(place == 0, place == lax.axis_size("dp") - 1)
            weight = jnp.where(ends, 0.0, 1.0)

        def total(at):
            value = sums_ref[:, at]
            if extra:
                value = value * weight
            for ref in refs[: len(extra)]:
                value = value + ref[:, at]
            return value

        col = beta_two * old_ref[...] + (1.0 - beta_two) * (total(pl.ds(0, cols)) / matrix_rows)
        col_out[...] = col
        scale_out[...] = lax.rsqrt(col)
        ratio = total(pl.ds(cols, cols)) / col
        update = ratio[:, :lanes]
        for k in range(1, cols // lanes):
            update = update + ratio[:, k * lanes : (k + 1) * lanes]
        update_out[...] = update
        mean_out[...] = total(pl.ds(2 * cols, lanes)) / matrix_rows

    return pl.pallas_call(
        body,
        out_shape=(f32(1, cols), f32(1, cols), f32(1, lanes), f32(1, lanes)),
        in_specs=[ON_CHIP] * (2 + len(extra)),
        out_specs=(ON_CHIP,) * 4,
        compiler_params=limits,
        cost_estimate=cost(cols, 4, 12),
        name="columns",
    )(sums, old_cols, *extra)


def select_run(choices, action):
    place = lax.axis_index("dp")
    for c, (places, _, _) in enumerate(choices):
        if len(choices) == 1:
            action(c)
        else:
            chosen = place == places[0]
            for other in places[1:]:
                chosen = jnp.logical_or(chosen, place == other)
            pl.when(chosen)(lambda c=c: action(c))


def apply_first(weights, choices, col_scale, row_mean, updates, matrix_rows, hidden_width):
    pieces = len(choices[0][1])
    count = pieces - 1
    rows, cols = choices[0][1][0].shape
    arrays = [array for _, gradient, new_row in choices for array in (*gradient[:count], *new_row)]
    each = count + pieces

    def body(weights_ref, col_ref, mean_ref, *refs):
        update_refs = refs[len(arrays) : len(arrays) + len(updates)]
        out_ref, factor_ref, scale_ref, held, sems = refs[-5:]
        update_total = update_refs[0][...]
        for ref in update_refs[1:]:
            update_total = update_total + ref[...]
        update_total = jnp.sum(update_total, axis=1, keepdims=True)
        row_mean = mean_ref[:, :1]
        clip_ratio = jnp.sqrt(update_total * row_mean / (matrix_rows * hidden_width))
        factor = step_rate * jnp.sqrt(row_mean) / jnp.maximum(1.0, clip_ratio)
        col_factor = factor * col_ref[...]
        factor_ref[...] = col_factor

        def copy(k):
            here = pl.ds(k * rows, rows)
            return pltpu.make_async_copy(held.at[here, :], out_ref.at[here, :], sems.at[k])

        for k in range(count):

            def write(c, k=k):
                here = pl.ds(k * rows, rows)
                row_scale = lax.rsqrt(refs[c * each + count + k][:, :1])
                held[here, :] = weights_ref[here, :] - refs[c * each + k][...] * row_scale * col_factor

            select_run(choices, write)
            copy(k).start()

        def last_scale(c):
            scale_ref[...] = lax.rsqrt(refs[c * each + count + pieces - 1][...])

        select_run(choices, last_scale)
        for k in range(count):
            copy(k).wait()

    return pl.pallas_call(
        body,
        out_shape=(f32(rows * pieces, cols), f32(1, cols), f32(rows, lanes)),
        in_specs=[ON_CHIP] * (3 + len(arrays) + len(updates)),
        out_specs=(IN_PLACE, ON_CHIP, ON_CHIP),
        scratch_shapes=[pltpu.VMEM((rows * count, cols), jnp.float32), pltpu.SemaphoreType.DMA((count,))],
        compiler_params=limits,
        cost_estimate=cost(rows * count * cols, 4, 12),
        name="apply",
    )(weights, col_scale, row_mean, *arrays, *updates)


def apply_last(weights, choices, begun, col_factor, row_scale):
    pieces = len(choices[0][1])
    rows, cols = choices[0][1][0].shape
    chunk = min(rows, 8)
    first = (pieces - 1) * rows
    arrays = [gradient[-1] for _, gradient, _ in choices]

    def body(weights_ref, factor_ref, scale_ref, *refs):
        out_ref, held, sems = refs[-3:]

        def copy(k):
            here = held.at[pl.ds(k * chunk, chunk), :]
            return pltpu.make_async_copy(here, out_ref.at[pl.ds(first + k * chunk, chunk), :], sems.at[k])

        def write(c):
            for k in range(rows // chunk):
                here = pl.ds(k * chunk, chunk)
                step = refs[c][here, :] * scale_ref[here, :1] * factor_ref[...]
                held[here, :] = weights_ref[first + k * chunk : first + (k + 1) * chunk, :] - step
                copy(k).start()

        select_run(choices, write)
        for k in range(rows // chunk):
            copy(k).wait()

    return pl.pallas_call(
        body,
        out_shape=f32(rows * pieces, cols),
        in_specs=[ON_CHIP] * (3 + len(arrays)) + [IN_PLACE],
        out_specs=IN_PLACE,
        scratch_shapes=[pltpu.VMEM((rows, cols), jnp.float32), pltpu.SemaphoreType.DMA((rows // chunk,))],
        input_output_aliases={3 + len(arrays): 0},
        compiler_params=limits,
        cost_estimate=cost(rows * cols, 3, 12),
        name="last",
    )(weights, col_factor, row_scale, *arrays, begun)


def row_line(choices):
    count = len(choices[0][2])
    rows = choices[0][2][0].shape[0]
    arrays = [array for _, _, new_row in choices for array in new_row]

    def body(*refs):
        place = lax.axis_index("dp")
        row = lax.broadcasted_iota(jnp.int32, (rows, lanes), 0)
        lane = lax.broadcasted_iota(jnp.int32, (rows, lanes), 1)
        line = jnp.zeros((1, lanes), jnp.float32)
        for piece in range(count):
            values = refs[piece][...]
            for c, (places, _, _) in enumerate(choices[1:], 1):
                for other in places:
                    values = jnp.where(place == other, refs[c * count + piece][...], values)
            at = lane == row + piece * rows
            line = line + jnp.sum(jnp.where(at, values, 0.0), axis=0, keepdims=True)
        refs[-1][...] = line

    return pl.pallas_call(
        body,
        out_shape=f32(1, lanes),
        in_specs=[ON_CHIP] * len(arrays),
        out_specs=ON_CHIP,
        compiler_params=limits,
        cost_estimate=cost(rows * count * lanes, 2, 4),
        name="rows",
    )(*arrays)


def short_line(grad, old_rows, hidden_width, pieces, rows):
    last = 3
    late = range(pieces // 2, pieces)
    soon = range(pieces // 2)
    order = [(2, p) for p in late] + [(3, p) for p in range(pieces)] + [(2, p) for p in soon]
    order += [(1, p) for p in soon] + [(1, p) for p in late]
    swap = [(0, 1), (1, 0), (2, 3), (3, 2)]
    middle = [(1, 2), (2, 1)]
    outward = [(0, 1), (3, 2)]
    ends = [0, last]

    def right(m):
        shard, piece = order[min(max(m, 0), len(order) - 1)]
        return shard * pieces + piece

    def left(m):
        shard, piece = order[min(max(m, 0), len(order) - 1)]
        return (last - shard) * pieces + piece

    P, M = {}, {}
    finished, new_row = {}, {}
    sums = []

    def own_table(slot):
        return [left(slot - 3), right(slot), left(slot), right(slot - 3)]

    def settle(slot, extra=()):
        table = own_table(slot)
        counted = [int(slot <= 8), int(slot >= 8), int(slot >= 8), int(slot <= 8)]
        arrived = [P[slot], M[slot]] if slot >= 8 else [P[slot]]
        gradient, row_part, col_part = finish_block(staged, table, arrived, rows)
        row_parts = [row_part] + other_parts(row_part, "col")
        finished[slot] = gradient
        carried = [new_row[3], new_row[4]] if slot == 8 else []
        new_row[slot], total = scale_block(
            gradient, table, counted, row_parts, old_rows, col_part, [*sums[-1:], *extra], carried, hidden_width
        )
        sums.append(total)

    for slot in range(10):
        if slot >= 2:
            operand = block_sum(staged, [0, right(slot - 2), left(slot - 2), 0], [P[slot - 2]], [], rows)
            M[slot] = lax.ppermute(operand, "dp", middle)
        table = [right(slot), left(slot - 3), right(slot - 3), left(slot)]
        arrived = [M[slot - 1]] if slot >= 3 else []
        if slot < 2:
            operand = fetch_block(grad, table, [1, 0, 0, 1], rows)
            staged = stage_gradient(grad, [operand])
        else:
            operand = block_sum(staged, table, arrived, [P[0]] if slot == 2 else [], rows)
        P[slot] = lax.ppermute(operand, "dp", swap)
        if 3 <= slot <= 8:
            settle(slot)
    early = lax.ppermute(sums[-1], "dp", outward)
    late_rows = unpack_rows(early, grad.shape[1], 2, rows)
    operand = pass_on(finished[3], [sums[-1]])
    P[10] = lax.ppermute(operand, "dp", outward)
    P[11] = lax.ppermute(pass_on(finished[4], [operand, early]), "dp", outward)
    settle(9, [early])
    total = axis_sum(sums[-1], "row")
    total = total + lax.ppermute(total, "dp", middle)
    extra = [lax.ppermute(total, "dp", [(1, 0), (2, 3)])]
    outer = ([finished[k] for k in range(5, 9)], [new_row[k] for k in range(5, 9)])
    inner = (
        [finished[8], finished[9], P[10], P[11]],
        [new_row[8], new_row[9], *late_rows],
    )
    return total, extra, [(ends, *outer), ([1, 2], *inner)]


def long_line(grad, old_rows, hidden_width, pieces, rows):
    replicas = lax.axis_size("dp")
    to_right = [(i, i + 1) for i in range(replicas - 1)]
    to_left = [(i + 1, i) for i in range(replicas - 1)]
    rights, lefts = {}, {}
    for slot in range((replicas - 1) * pieces):
        step, piece = divmod(slot, pieces)
        right_table = [min(replicas - 1 - step + z, replicas - 1) * pieces + piece for z in range(replicas)]
        left_table = [max(step - (replicas - 1) + z, 0) * pieces + piece for z in range(replicas)]
        before = slot - pieces
        right = block_sum(grad, right_table, [rights[before]] if step else [], [], rows)
        left = block_sum(grad, left_table, [lefts[before]] if step else [], [], rows)
        rights[slot] = lax.ppermute(right, "dp", to_right[: step + 1])
        lefts[slot] = lax.ppermute(left, "dp", to_left[replicas - 2 - step :])
    gradient, new_row, held = [], [], []
    for piece in range(pieces):
        slot = (replicas - 2) * pieces + piece
        table = [z * pieces + piece for z in range(replicas)]
        grad_piece, row_part, col_part = finish_block(grad, table, [rights[slot], lefts[slot]], rows)
        row_parts = [row_part] + other_parts(row_part, "col")
        row_piece, sums = scale_block(
            grad_piece, table, [1] * replicas, row_parts, old_rows, col_part, held, [], hidden_width
        )
        held = [sums]
        gradient.append(grad_piece)
        new_row.append(row_piece)
    total = axis_sum(axis_sum(sums, "row"), "dp")
    return total, [], [(list(range(replicas)), gradient, new_row)]


def shards(grad_parts, params, row_second, col_second):
    owned_rows = params.shape[2]
    local_cols = params.shape[3]
    slab_rows = row_second.shape[2]
    hidden_width = local_cols * lax.axis_size("col")
    matrix_rows = slab_rows * lax.axis_size("row")
    replicas = lax.axis_size("dp")
    pieces = 4 if owned_rows >= 64 else 2
    rows = owned_rows // pieces
    grad = grad_parts.reshape(slab_rows, local_cols)
    weights = params.reshape(owned_rows, local_cols)
    old_rows = jnp.broadcast_to(row_second.reshape(slab_rows, 1), (slab_rows, lanes))
    old_cols = col_second.reshape(1, local_cols)
    line = short_line if replicas == 4 and pieces == 4 else long_line
    total, extra, choices = line(grad, old_rows, hidden_width, pieces, rows)
    new_col, col_scale, update_part, row_mean = column_factor(total, extra, old_cols, matrix_rows)
    updates = [update_part] + other_parts(update_part, "col")
    begun, col_factor, row_scale = apply_first(
        weights, choices, col_scale, row_mean, updates, matrix_rows, hidden_width
    )
    new_params = apply_last(weights, choices, begun, col_factor, row_scale)
    new_row = row_line(choices)[:, :owned_rows]
    return (new_params.reshape(params.shape), new_row.reshape(1, 1, owned_rows), new_col)


def solution(mesh):
    return jax.shard_map(
        shards,
        mesh=mesh,
        in_specs=(
            P("dp", None, "row", None, "col"),
            P(None, "row", "dp", "col"),
            P(None, "row", None),
            P(None, "col"),
        ),
        out_specs=(P(None, "row", "dp", "col"), P(None, "row", "dp"), P(None, "col")),
        check_vma=False,
    )
```

```python
import jax
import jax.numpy as jnp
from jax import lax
from jax.experimental import pallas as pl
from jax.experimental.pallas import tpu as pltpu
from jax.sharding import PartitionSpec as P

beta_two = 1.0 - 8.0 ** (-0.8)
step_rate = 0.5
tiny_add = 1e-30
lanes = 128
ON_CHIP = pl.BlockSpec(memory_space=pltpu.VMEM)
IN_PLACE = pl.BlockSpec(memory_space=pltpu.HBM)
limits = pltpu.CompilerParams(vmem_limit_bytes=8 * 1024 * 1024)


def f32(*shape):
    return jax.ShapeDtypeStruct(shape, jnp.float32)


def cost(elements, flops, width):
    return pl.CostEstimate(flops=flops * elements, bytes_accessed=width * elements, transcendentals=0)


def axis_sum(values, axis):
    size = lax.axis_size(axis)
    hop = 1
    while hop < size:
        pairs = [(i, i ^ hop) for i in range(size)]
        values = values + lax.ppermute(values, axis, pairs)
        hop *= 2
    return values


def other_parts(values, axis):
    size = lax.axis_size(axis)
    return [lax.ppermute(values, axis, [(i, (i + k) % size) for i in range(size)]) for k in range(1, size)]


def pick(table):
    place = lax.axis_index("dp")
    value = jnp.int32(table[0])
    for k in range(1, len(table)):
        value = jnp.where(place == k, jnp.int32(table[k]), value)
    return value


def block_sum(grad, table, arrived, tokens, rows):
    cols = grad.shape[1]

    def body(grad_ref, *refs):
        start = pl.multiple_of(pick(table) * rows, rows)
        values = grad_ref[pl.ds(start, rows), :].astype(jnp.float32)
        for ref in refs[: len(arrived)]:
            values = values + ref[...]
        refs[-1][...] = values

    return pl.pallas_call(
        body,
        out_shape=f32(rows, cols),
        in_specs=[ON_CHIP] * (1 + len(arrived) + len(tokens)),
        out_specs=ON_CHIP,
        compiler_params=limits,
        cost_estimate=cost(rows * cols, 1, 10),
        name="block",
    )(grad, *arrived, *tokens)


def stage_gradient(grad, tokens):
    def body(grad_ref, *refs):
        out_ref, sem = refs[-2:]
        copy = pltpu.make_async_copy(grad_ref, out_ref, sem)
        copy.start()
        copy.wait()

    return pl.pallas_call(
        body,
        out_shape=jax.ShapeDtypeStruct(grad.shape, grad.dtype),
        in_specs=[IN_PLACE] + [ON_CHIP] * len(tokens),
        out_specs=ON_CHIP,
        scratch_shapes=[pltpu.SemaphoreType.DMA(())],
        compiler_params=limits,
        cost_estimate=cost(grad.size, 0, 2),
        name="stage",
    )(pltpu.with_memory_space_constraint(grad, pltpu.HBM), *tokens)


def fetch_block(grad, table, places, rows):
    cols = grad.shape[1]
    chunk = min(rows, 8)

    def body(grad_ref, out_ref, held, sems):
        wanted = pick(places) > 0
        start = pick(table) * rows

        def copy(k):
            at = pl.ds(pl.multiple_of(start + k * chunk, chunk), chunk)
            return pltpu.make_async_copy(grad_ref.at[at, :], held.at[pl.ds(k * chunk, chunk), :], sems.at[k])

        @pl.when(wanted)
        def _():
            for k in range(rows // chunk):
                copy(k).start()
            for k in range(rows // chunk):
                at = pl.ds(k * chunk, chunk)
                copy(k).wait()
                out_ref[at, :] = held[at, :].astype(jnp.float32)

        @pl.when(jnp.logical_not(wanted))
        def _():
            out_ref[...] = jnp.zeros((rows, cols), jnp.float32)

    return pl.pallas_call(
        body,
        out_shape=f32(rows, cols),
        in_specs=[IN_PLACE],
        out_specs=ON_CHIP,
        scratch_shapes=[pltpu.VMEM((rows, cols), grad.dtype), pltpu.SemaphoreType.DMA((rows // chunk,))],
        compiler_params=limits,
        cost_estimate=cost(rows * cols, 1, 6),
        name="fetch",
    )(pltpu.with_memory_space_constraint(grad, pltpu.HBM))


def pass_on(values, tokens):
    def body(values_ref, *refs):
        refs[-1][...] = values_ref[...]

    return pl.pallas_call(
        body,
        out_shape=f32(*values.shape),
        in_specs=[ON_CHIP] * (1 + len(tokens)),
        out_specs=ON_CHIP,
        compiler_params=limits,
        cost_estimate=cost(values.size, 1, 8),
        name="pass",
    )(values, *tokens)


def finish_block(grad, table, arrived, rows):
    cols = arrived[0].shape[1]

    def body(grad_ref, *refs):
        out_ref, row_ref, col_ref = refs[-3:]
        start = pl.multiple_of(pick(table) * rows, rows)
        for k in range(cols // lanes):
            at = pl.ds(k * lanes, lanes)
            values = grad_ref[pl.ds(start, rows), at].astype(jnp.float32)
            for ref in refs[: len(arrived)]:
                values = values + ref[:, at]
            out_ref[:, at] = values
            squares = values * values + tiny_add
            row_part = squares if k == 0 else row_part + squares
            col_ref[:, at] = jnp.sum(squares, axis=0, keepdims=True)
        row_ref[...] = row_part

    return pl.pallas_call(
        body,
        out_shape=(f32(rows, cols), f32(rows, lanes), f32(1, cols)),
        in_specs=[ON_CHIP] * (1 + len(arrived)),
        out_specs=(ON_CHIP,) * 3,
        compiler_params=limits,
        cost_estimate=cost(rows * cols, 6, 14),
        name="finish",
    )(grad, *arrived)


def diagonal(rows):
    row = lax.broadcasted_iota(jnp.int32, (rows, lanes), 0)
    return row == lax.broadcasted_iota(jnp.int32, (rows, lanes), 1)


def half_of(side, cols, k):
    return pl.ds(pl.multiple_of(side * (cols // 2) + k * lanes, lanes), lanes)


def other_half(sums, cols):
    def body(sums_ref, out_ref):
        side = 1 - lax.rem(lax.axis_index("row"), 2)
        for k in range(cols // 2 // lanes):
            out_ref[:, pl.ds(k * lanes, lanes)] = sums_ref[:, half_of(side, cols, k)]
            out_ref[:, pl.ds(cols // 2 + k * lanes, lanes)] = sums_ref[:, half_of(side + 2, cols, k)]

    return pl.pallas_call(
        body,
        out_shape=f32(1, cols),
        in_specs=[ON_CHIP],
        out_specs=ON_CHIP,
        compiler_params=limits,
        cost_estimate=cost(cols, 1, 8),
        name="half",
    )(sums)


def joined_half(sums, received, cols):
    width = sums.shape[1] - cols

    def body(sums_ref, received_ref, out_ref):
        side = lax.rem(lax.axis_index("row"), 2)
        for k in range(cols // 2 // lanes):
            at = pl.ds(k * lanes, lanes)
            out_ref[:, at] = sums_ref[:, half_of(side, cols, k)] + received_ref[:, at]
            at = pl.ds(cols // 2 + k * lanes, lanes)
            out_ref[:, at] = sums_ref[:, half_of(side + 2, cols, k)] + received_ref[:, at]
        out_ref[:, cols:width] = sums_ref[:, 2 * cols : cols + width]

    return pl.pallas_call(
        body,
        out_shape=f32(1, width),
        in_specs=[ON_CHIP] * 2,
        out_specs=ON_CHIP,
        compiler_params=limits,
        cost_estimate=cost(cols, 1, 12),
        name="joined",
    )(sums, received)


def unpack_rows(sums, cols, count, rows):
    def body(sums_ref, *outs):
        for k, out in enumerate(outs):
            values = sums_ref[:, pl.ds(cols + (k + 1) * lanes, lanes)]
            column = jnp.sum(jnp.where(diagonal(rows), values, 0.0), axis=1, keepdims=True)
            out[...] = jnp.broadcast_to(column, (rows, lanes))

    return pl.pallas_call(
        body,
        out_shape=(f32(rows, lanes),) * count,
        in_specs=[ON_CHIP],
        out_specs=(ON_CHIP,) * count,
        compiler_params=limits,
        cost_estimate=cost(rows * lanes, 2, 8),
        name="unpack",
    )(sums)


def scale_block(gradient, table, counted, row_parts, old_rows, col_part, held, halves, carried, hidden_width):
    rows, cols = gradient.shape

    def body(grad_ref, col_ref, old_ref, *refs):
        row_out, sums_out = refs[-2:]
        total = refs[0][...]
        for ref in refs[1 : len(row_parts)]:
            total = total + ref[...]
        row_sum = jnp.sum(total, axis=1, keepdims=True)
        old = old_ref[pl.ds(pl.multiple_of(pick(table) * rows, rows), rows), :]
        row = beta_two * old + (1.0 - beta_two) * (row_sum / hidden_width)
        row_out[...] = row
        inverse = 1.0 / row
        before = refs[len(row_parts) : len(row_parts) + len(held)]
        counts = pick(counted) > 0

        def put(at, value):
            value = jnp.where(counts, value, 0.0)
            for ref in before:
                value = value + ref[:, at]
            sums_out[:, at] = value

        put(pl.ds(2 * cols, lanes), jnp.sum(row, axis=0, keepdims=True))
        for k in range(len(carried)):
            values = refs[len(row_parts) + len(held) + len(halves) + k][...]
            at = pl.ds(2 * cols + (k + 1) * lanes, lanes)
            sums_out[:, at] = jnp.sum(jnp.where(diagonal(rows), values, 0.0), axis=0, keepdims=True)
        for k in range(cols // lanes):
            at = pl.ds(k * lanes, lanes)
            values = grad_ref[:, at]
            put(at, col_ref[:, at])
            put(pl.ds(cols + k * lanes, lanes), jnp.sum(values * values * inverse, axis=0, keepdims=True))
        for half in refs[len(row_parts) + len(held) : len(row_parts) + len(held) + len(halves)]:
            side = lax.rem(lax.axis_index("row"), 2)
            for k in range(cols // 2 // lanes):
                sums_out[:, half_of(side, cols, k)] += half[:, pl.ds(k * lanes, lanes)]
                sums_out[:, half_of(side + 2, cols, k)] += half[:, pl.ds(cols // 2 + k * lanes, lanes)]
            sums_out[:, pl.ds(2 * cols, lanes)] += half[:, pl.ds(cols, lanes)]

    return pl.pallas_call(
        body,
        out_shape=(f32(rows, lanes), f32(1, 2 * cols + (1 + len(carried)) * lanes)),
        in_specs=[ON_CHIP] * (3 + len(row_parts) + len(held) + len(halves) + len(carried)),
        out_specs=(ON_CHIP, ON_CHIP),
        compiler_params=limits,
        cost_estimate=cost(rows * cols, 4, 4),
        name="scale",
    )(gradient, col_part, old_rows, *row_parts, *held, *halves, *carried)


def column_factor(sums, extra, old_cols, matrix_rows):
    cols = old_cols.shape[1]

    def body(sums_ref, old_ref, *refs):
        col_out, scale_out, update_out, mean_out = refs[-4:]
        weight = 1.0
        if extra:
            place = lax.axis_index("dp")
            ends = jnp.logical_or(place == 0, place == lax.axis_size("dp") - 1)
            weight = jnp.where(ends, 0.0, 1.0)

        def total(at):
            value = sums_ref[:, at]
            if extra:
                value = value * weight
            for ref in refs[: len(extra)]:
                value = value + ref[:, at]
            return value

        col = beta_two * old_ref[...] + (1.0 - beta_two) * (total(pl.ds(0, cols)) / matrix_rows)
        col_out[...] = col
        scale_out[...] = lax.rsqrt(col)
        ratio = total(pl.ds(cols, cols)) / col
        update = ratio[:, :lanes]
        for k in range(1, cols // lanes):
            update = update + ratio[:, k * lanes : (k + 1) * lanes]
        update_out[...] = update
        mean_out[...] = total(pl.ds(2 * cols, lanes)) / matrix_rows

    return pl.pallas_call(
        body,
        out_shape=(f32(1, cols), f32(1, cols), f32(1, lanes), f32(1, lanes)),
        in_specs=[ON_CHIP] * (2 + len(extra)),
        out_specs=(ON_CHIP,) * 4,
        compiler_params=limits,
        cost_estimate=cost(cols, 4, 12),
        name="columns",
    )(sums, old_cols, *extra)


def select_run(choices, action):
    place = lax.axis_index("dp")
    for c, (places, _, _) in enumerate(choices):
        if len(choices) == 1:
            action(c)
        else:
            chosen = place == places[0]
            for other in places[1:]:
                chosen = jnp.logical_or(chosen, place == other)
            pl.when(chosen)(lambda c=c: action(c))


def apply_first(weights, choices, col_scale, row_mean, updates, matrix_rows, hidden_width):
    pieces = len(choices[0][1])
    count = pieces - 1
    rows, cols = choices[0][1][0].shape
    arrays = [array for _, gradient, new_row in choices for array in (*gradient[:count], *new_row)]
    each = count + pieces

    def body(weights_ref, col_ref, mean_ref, *refs):
        update_refs = refs[len(arrays) : len(arrays) + len(updates)]
        out_ref, factor_ref, scale_ref, held, sems = refs[-5:]
        update_total = update_refs[0][...]
        for ref in update_refs[1:]:
            update_total = update_total + ref[...]
        update_total = jnp.sum(update_total, axis=1, keepdims=True)
        row_mean = mean_ref[:, :1]
        clip_ratio = jnp.sqrt(update_total * row_mean / (matrix_rows * hidden_width))
        factor = step_rate * jnp.sqrt(row_mean) / jnp.maximum(1.0, clip_ratio)
        col_factor = factor * col_ref[...]
        factor_ref[...] = col_factor

        def copy(k):
            here = pl.ds(k * rows, rows)
            return pltpu.make_async_copy(held.at[here, :], out_ref.at[here, :], sems.at[k])

        for k in range(count):

            def write(c, k=k):
                here = pl.ds(k * rows, rows)
                row_scale = lax.rsqrt(refs[c * each + count + k][:, :1])
                held[here, :] = weights_ref[here, :] - refs[c * each + k][...] * row_scale * col_factor

            select_run(choices, write)
            copy(k).start()

        def last_scale(c):
            scale_ref[...] = lax.rsqrt(refs[c * each + count + pieces - 1][...])

        select_run(choices, last_scale)
        for k in range(count):
            copy(k).wait()

    return pl.pallas_call(
        body,
        out_shape=(f32(rows * pieces, cols), f32(1, cols), f32(rows, lanes)),
        in_specs=[ON_CHIP] * (3 + len(arrays) + len(updates)),
        out_specs=(IN_PLACE, ON_CHIP, ON_CHIP),
        scratch_shapes=[pltpu.VMEM((rows * count, cols), jnp.float32), pltpu.SemaphoreType.DMA((count,))],
        compiler_params=limits,
        cost_estimate=cost(rows * count * cols, 4, 12),
        name="apply",
    )(weights, col_scale, row_mean, *arrays, *updates)


def apply_last(weights, choices, begun, col_factor, row_scale):
    pieces = len(choices[0][1])
    rows, cols = choices[0][1][0].shape
    chunk = min(rows, 8)
    first = (pieces - 1) * rows
    arrays = [gradient[-1] for _, gradient, _ in choices]

    def body(weights_ref, factor_ref, scale_ref, *refs):
        out_ref, held, sems = refs[-3:]

        def copy(k):
            here = held.at[pl.ds(k * chunk, chunk), :]
            return pltpu.make_async_copy(here, out_ref.at[pl.ds(first + k * chunk, chunk), :], sems.at[k])

        def write(c):
            for k in range(rows // chunk):
                here = pl.ds(k * chunk, chunk)
                step = refs[c][here, :] * scale_ref[here, :1] * factor_ref[...]
                held[here, :] = weights_ref[first + k * chunk : first + (k + 1) * chunk, :] - step
                copy(k).start()

        select_run(choices, write)
        for k in range(rows // chunk):
            copy(k).wait()

    return pl.pallas_call(
        body,
        out_shape=f32(rows * pieces, cols),
        in_specs=[ON_CHIP] * (3 + len(arrays)) + [IN_PLACE],
        out_specs=IN_PLACE,
        scratch_shapes=[pltpu.VMEM((rows, cols), jnp.float32), pltpu.SemaphoreType.DMA((rows // chunk,))],
        input_output_aliases={3 + len(arrays): 0},
        compiler_params=limits,
        cost_estimate=cost(rows * cols, 3, 12),
        name="last",
    )(weights, col_factor, row_scale, *arrays, begun)


def row_line(choices):
    count = len(choices[0][2])
    rows = choices[0][2][0].shape[0]
    arrays = [array for _, _, new_row in choices for array in new_row]

    def body(*refs):
        place = lax.axis_index("dp")
        row = lax.broadcasted_iota(jnp.int32, (rows, lanes), 0)
        lane = lax.broadcasted_iota(jnp.int32, (rows, lanes), 1)
        line = jnp.zeros((1, lanes), jnp.float32)
        for piece in range(count):
            values = refs[piece][...]
            for c, (places, _, _) in enumerate(choices[1:], 1):
                for other in places:
                    values = jnp.where(place == other, refs[c * count + piece][...], values)
            at = lane == row + piece * rows
            line = line + jnp.sum(jnp.where(at, values, 0.0), axis=0, keepdims=True)
        refs[-1][...] = line

    return pl.pallas_call(
        body,
        out_shape=f32(1, lanes),
        in_specs=[ON_CHIP] * len(arrays),
        out_specs=ON_CHIP,
        compiler_params=limits,
        cost_estimate=cost(rows * count * lanes, 2, 4),
        name="rows",
    )(*arrays)


def short_line(grad, old_rows, hidden_width, pieces, rows):
    last = 3
    late = range(pieces // 2, pieces)
    soon = range(pieces // 2)
    order = [(2, p) for p in late] + [(3, p) for p in range(pieces)] + [(2, p) for p in soon]
    order += [(1, p) for p in soon] + [(1, p) for p in late]
    swap = [(0, 1), (1, 0), (2, 3), (3, 2)]
    middle = [(1, 2), (2, 1)]
    outward = [(0, 1), (3, 2)]
    ends = [0, last]

    def right(m):
        shard, piece = order[min(max(m, 0), len(order) - 1)]
        return shard * pieces + piece

    def left(m):
        shard, piece = order[min(max(m, 0), len(order) - 1)]
        return (last - shard) * pieces + piece

    P, M = {}, {}
    finished, new_row = {}, {}
    sums = []

    def own_table(slot):
        return [left(slot - 3), right(slot), left(slot), right(slot - 3)]

    def settle(slot, extra=()):
        table = own_table(slot)
        counted = [int(slot <= 8), int(slot >= 8), int(slot >= 8), int(slot <= 8)]
        arrived = [P[slot], M[slot]] if slot >= 8 else [P[slot]]
        gradient, row_part, col_part = finish_block(staged, table, arrived, rows)
        row_parts = [row_part] + other_parts(row_part, "col")
        finished[slot] = gradient
        carried = [new_row[3], new_row[4]] if slot == 8 else []
        new_row[slot], total = scale_block(
            gradient, table, counted, row_parts, old_rows, col_part, sums[-1:], list(extra), carried, hidden_width
        )
        sums.append(total)

    for slot in range(10):
        if slot >= 2:
            operand = block_sum(staged, [0, right(slot - 2), left(slot - 2), 0], [P[slot - 2]], [], rows)
            M[slot] = lax.ppermute(operand, "dp", middle)
        table = [right(slot), left(slot - 3), right(slot - 3), left(slot)]
        arrived = [M[slot - 1]] if slot >= 3 else []
        if slot < 2:
            operand = fetch_block(grad, table, [1, 0, 0, 1], rows)
            staged = stage_gradient(grad, [operand])
        else:
            operand = block_sum(staged, table, arrived, [P[0]] if slot == 2 else [], rows)
        P[slot] = lax.ppermute(operand, "dp", swap)
        if 3 <= slot <= 8:
            settle(slot)
    cols = grad.shape[1]
    side = lax.axis_size("row")
    received = lax.ppermute(other_half(sums[-1], cols), "row", [(i, i ^ 1) for i in range(side)])
    early = lax.ppermute(joined_half(sums[-1], received, cols), "dp", outward)
    late_rows = unpack_rows(early, grad.shape[1], 2, rows)
    operand = pass_on(finished[3], [sums[-1]])
    P[10] = lax.ppermute(operand, "dp", outward)
    P[11] = lax.ppermute(pass_on(finished[4], [operand, early]), "dp", outward)
    settle(9, [early])
    total = axis_sum(sums[-1], "row")
    total = total + lax.ppermute(total, "dp", middle)
    extra = [lax.ppermute(total, "dp", [(1, 0), (2, 3)])]
    outer = ([finished[k] for k in range(5, 9)], [new_row[k] for k in range(5, 9)])
    inner = (
        [finished[8], finished[9], P[10], P[11]],
        [new_row[8], new_row[9], *late_rows],
    )
    return total, extra, [(ends, *outer), ([1, 2], *inner)]


def long_line(grad, old_rows, hidden_width, pieces, rows):
    replicas = lax.axis_size("dp")
    to_right = [(i, i + 1) for i in range(replicas - 1)]
    to_left = [(i + 1, i) for i in range(replicas - 1)]
    rights, lefts = {}, {}
    for slot in range((replicas - 1) * pieces):
        step, piece = divmod(slot, pieces)
        right_table = [min(replicas - 1 - step + z, replicas - 1) * pieces + piece for z in range(replicas)]
        left_table = [max(step - (replicas - 1) + z, 0) * pieces + piece for z in range(replicas)]
        before = slot - pieces
        right = block_sum(grad, right_table, [rights[before]] if step else [], [], rows)
        left = block_sum(grad, left_table, [lefts[before]] if step else [], [], rows)
        rights[slot] = lax.ppermute(right, "dp", to_right[: step + 1])
        lefts[slot] = lax.ppermute(left, "dp", to_left[replicas - 2 - step :])
    gradient, new_row, held = [], [], []
    for piece in range(pieces):
        slot = (replicas - 2) * pieces + piece
        table = [z * pieces + piece for z in range(replicas)]
        grad_piece, row_part, col_part = finish_block(grad, table, [rights[slot], lefts[slot]], rows)
        row_parts = [row_part] + other_parts(row_part, "col")
        row_piece, sums = scale_block(
            grad_piece, table, [1] * replicas, row_parts, old_rows, col_part, held, [], [], hidden_width
        )
        held = [sums]
        gradient.append(grad_piece)
        new_row.append(row_piece)
    total = axis_sum(axis_sum(sums, "row"), "dp")
    return total, [], [(list(range(replicas)), gradient, new_row)]


def shards(grad_parts, params, row_second, col_second):
    owned_rows = params.shape[2]
    local_cols = params.shape[3]
    slab_rows = row_second.shape[2]
    hidden_width = local_cols * lax.axis_size("col")
    matrix_rows = slab_rows * lax.axis_size("row")
    replicas = lax.axis_size("dp")
    pieces = 4 if owned_rows >= 64 else 2
    rows = owned_rows // pieces
    grad = grad_parts.reshape(slab_rows, local_cols)
    weights = params.reshape(owned_rows, local_cols)
    old_rows = jnp.broadcast_to(row_second.reshape(slab_rows, 1), (slab_rows, lanes))
    old_cols = col_second.reshape(1, local_cols)
    short = replicas == 4 and pieces == 4 and lax.axis_size("row") % 2 == 0 and local_cols % (2 * lanes) == 0
    line = short_line if short else long_line
    total, extra, choices = line(grad, old_rows, hidden_width, pieces, rows)
    new_col, col_scale, update_part, row_mean = column_factor(total, extra, old_cols, matrix_rows)
    updates = [update_part] + other_parts(update_part, "col")
    begun, col_factor, row_scale = apply_first(
        weights, choices, col_scale, row_mean, updates, matrix_rows, hidden_width
    )
    new_params = apply_last(weights, choices, begun, col_factor, row_scale)
    new_row = row_line(choices)[:, :owned_rows]
    return (new_params.reshape(params.shape), new_row.reshape(1, 1, owned_rows), new_col)


def solution(mesh):
    return jax.shard_map(
        shards,
        mesh=mesh,
        in_specs=(
            P("dp", None, "row", None, "col"),
            P(None, "row", "dp", "col"),
            P(None, "row", None),
            P(None, "col"),
        ),
        out_specs=(P(None, "row", "dp", "col"), P(None, "row", "dp"), P(None, "col")),
        check_vma=False,
    )
```

```python
import jax
import jax.numpy as jnp
from jax import lax
from jax.experimental import pallas as pl
from jax.experimental.pallas import tpu as pltpu
from jax.sharding import PartitionSpec as P

beta_two = 1.0 - 8.0 ** (-0.8)
step_rate = 0.5
tiny_add = 1e-30
lanes = 128
ON_CHIP = pl.BlockSpec(memory_space=pltpu.VMEM)
IN_PLACE = pl.BlockSpec(memory_space=pltpu.HBM)
limits = pltpu.CompilerParams(vmem_limit_bytes=8 * 1024 * 1024)


def f32(*shape):
    return jax.ShapeDtypeStruct(shape, jnp.float32)


def cost(elements, flops, width):
    return pl.CostEstimate(flops=flops * elements, bytes_accessed=width * elements, transcendentals=0)


def axis_sum(values, axis):
    size = lax.axis_size(axis)
    hop = 1
    while hop < size:
        pairs = [(i, i ^ hop) for i in range(size)]
        values = values + lax.ppermute(values, axis, pairs)
        hop *= 2
    return values


def other_parts(values, axis):
    size = lax.axis_size(axis)
    return [lax.ppermute(values, axis, [(i, (i + k) % size) for i in range(size)]) for k in range(1, size)]


def pick(table):
    place = lax.axis_index("dp")
    value = jnp.int32(table[0])
    for k in range(1, len(table)):
        value = jnp.where(place == k, jnp.int32(table[k]), value)
    return value


def block_sum(grad, table, arrived, tokens, rows):
    cols = grad.shape[1]

    def body(grad_ref, *refs):
        start = pl.multiple_of(pick(table) * rows, rows)
        values = grad_ref[pl.ds(start, rows), :].astype(jnp.float32)
        for ref in refs[: len(arrived)]:
            values = values + ref[...]
        refs[-1][...] = values

    return pl.pallas_call(
        body,
        out_shape=f32(rows, cols),
        in_specs=[ON_CHIP] * (1 + len(arrived) + len(tokens)),
        out_specs=ON_CHIP,
        compiler_params=limits,
        cost_estimate=cost(rows * cols, 1, 10),
        name="block",
    )(grad, *arrived, *tokens)


def stage_gradient(grad, tokens):
    def body(grad_ref, *refs):
        out_ref, sem = refs[-2:]
        copy = pltpu.make_async_copy(grad_ref, out_ref, sem)
        copy.start()
        copy.wait()

    return pl.pallas_call(
        body,
        out_shape=jax.ShapeDtypeStruct(grad.shape, grad.dtype),
        in_specs=[IN_PLACE] + [ON_CHIP] * len(tokens),
        out_specs=ON_CHIP,
        scratch_shapes=[pltpu.SemaphoreType.DMA(())],
        compiler_params=limits,
        cost_estimate=cost(grad.size, 0, 2),
        name="stage",
    )(pltpu.with_memory_space_constraint(grad, pltpu.HBM), *tokens)


def fetch_block(grad, table, places, rows):
    cols = grad.shape[1]
    chunk = min(rows, 8)

    def body(grad_ref, out_ref, held, sems):
        wanted = pick(places) > 0
        start = pick(table) * rows

        def copy(k):
            at = pl.ds(pl.multiple_of(start + k * chunk, chunk), chunk)
            return pltpu.make_async_copy(grad_ref.at[at, :], held.at[pl.ds(k * chunk, chunk), :], sems.at[k])

        @pl.when(wanted)
        def _():
            for k in range(rows // chunk):
                copy(k).start()
            for k in range(rows // chunk):
                at = pl.ds(k * chunk, chunk)
                copy(k).wait()
                out_ref[at, :] = held[at, :].astype(jnp.float32)

        @pl.when(jnp.logical_not(wanted))
        def _():
            out_ref[...] = jnp.zeros((rows, cols), jnp.float32)

    return pl.pallas_call(
        body,
        out_shape=f32(rows, cols),
        in_specs=[IN_PLACE],
        out_specs=ON_CHIP,
        scratch_shapes=[pltpu.VMEM((rows, cols), grad.dtype), pltpu.SemaphoreType.DMA((rows // chunk,))],
        compiler_params=limits,
        cost_estimate=cost(rows * cols, 1, 6),
        name="fetch",
    )(pltpu.with_memory_space_constraint(grad, pltpu.HBM))


def pass_on(values, tokens):
    def body(values_ref, *refs):
        refs[-1][...] = values_ref[...]

    return pl.pallas_call(
        body,
        out_shape=f32(*values.shape),
        in_specs=[ON_CHIP] * (1 + len(tokens)),
        out_specs=ON_CHIP,
        compiler_params=limits,
        cost_estimate=cost(values.size, 1, 8),
        name="pass",
    )(values, *tokens)


def finish_block(grad, table, arrived, rows):
    cols = arrived[0].shape[1]

    def body(grad_ref, *refs):
        out_ref, row_ref, col_ref = refs[-3:]
        start = pl.multiple_of(pick(table) * rows, rows)
        for k in range(cols // lanes):
            at = pl.ds(k * lanes, lanes)
            values = grad_ref[pl.ds(start, rows), at].astype(jnp.float32)
            for ref in refs[: len(arrived)]:
                values = values + ref[:, at]
            out_ref[:, at] = values
            squares = values * values + tiny_add
            row_part = squares if k == 0 else row_part + squares
            col_ref[:, at] = jnp.sum(squares, axis=0, keepdims=True)
        row_ref[...] = row_part

    return pl.pallas_call(
        body,
        out_shape=(f32(rows, cols), f32(rows, lanes), f32(1, cols)),
        in_specs=[ON_CHIP] * (1 + len(arrived)),
        out_specs=(ON_CHIP,) * 3,
        compiler_params=limits,
        cost_estimate=cost(rows * cols, 6, 14),
        name="finish",
    )(grad, *arrived)


def diagonal(rows):
    row = lax.broadcasted_iota(jnp.int32, (rows, lanes), 0)
    return row == lax.broadcasted_iota(jnp.int32, (rows, lanes), 1)


def half_of(side, cols, k):
    return pl.ds(pl.multiple_of(side * (cols // 2) + k * lanes, lanes), lanes)


def other_half(sums, cols):
    def body(sums_ref, out_ref):
        side = 1 - lax.rem(lax.axis_index("row"), 2)
        for k in range(cols // 2 // lanes):
            out_ref[:, pl.ds(k * lanes, lanes)] = sums_ref[:, half_of(side, cols, k)]
            out_ref[:, pl.ds(cols // 2 + k * lanes, lanes)] = sums_ref[:, half_of(side + 2, cols, k)]

    return pl.pallas_call(
        body,
        out_shape=f32(1, cols),
        in_specs=[ON_CHIP],
        out_specs=ON_CHIP,
        compiler_params=limits,
        cost_estimate=cost(cols, 1, 8),
        name="half",
    )(sums)


def joined_half(sums, received, cols):
    width = sums.shape[1] - cols

    def body(sums_ref, received_ref, out_ref):
        side = lax.rem(lax.axis_index("row"), 2)
        for k in range(cols // 2 // lanes):
            at = pl.ds(k * lanes, lanes)
            out_ref[:, at] = sums_ref[:, half_of(side, cols, k)] + received_ref[:, at]
            at = pl.ds(cols // 2 + k * lanes, lanes)
            out_ref[:, at] = sums_ref[:, half_of(side + 2, cols, k)] + received_ref[:, at]
        out_ref[:, cols:width] = sums_ref[:, 2 * cols : cols + width]

    return pl.pallas_call(
        body,
        out_shape=f32(1, width),
        in_specs=[ON_CHIP] * 2,
        out_specs=ON_CHIP,
        compiler_params=limits,
        cost_estimate=cost(cols, 1, 12),
        name="joined",
    )(sums, received)


def unpack_rows(sums, cols, count, rows):
    def body(sums_ref, *outs):
        for k, out in enumerate(outs):
            values = sums_ref[:, pl.ds(cols + (k + 1) * lanes, lanes)]
            column = jnp.sum(jnp.where(diagonal(rows), values, 0.0), axis=1, keepdims=True)
            out[...] = jnp.broadcast_to(column, (rows, lanes))

    return pl.pallas_call(
        body,
        out_shape=(f32(rows, lanes),) * count,
        in_specs=[ON_CHIP],
        out_specs=(ON_CHIP,) * count,
        compiler_params=limits,
        cost_estimate=cost(rows * lanes, 2, 8),
        name="unpack",
    )(sums)


def scale_block(gradient, table, counted, row_parts, old_rows, col_part, held, halves, carried, hidden_width):
    rows, cols = gradient.shape

    def body(grad_ref, col_ref, old_ref, *refs):
        row_out, sums_out = refs[-2:]
        total = refs[0][...]
        for ref in refs[1 : len(row_parts)]:
            total = total + ref[...]
        row_sum = jnp.sum(total, axis=1, keepdims=True)
        old = old_ref[pl.ds(pl.multiple_of(pick(table) * rows, rows), rows), :]
        row = beta_two * old + (1.0 - beta_two) * (row_sum / hidden_width)
        row_out[...] = row
        inverse = 1.0 / row
        before = refs[len(row_parts) : len(row_parts) + len(held)]
        counts = pick(counted) > 0

        def put(at, value):
            value = jnp.where(counts, value, 0.0)
            for ref in before:
                value = value + ref[:, at]
            sums_out[:, at] = value

        put(pl.ds(2 * cols, lanes), jnp.sum(row, axis=0, keepdims=True))
        for k in range(len(carried)):
            values = refs[len(row_parts) + len(held) + len(halves) + k][...]
            at = pl.ds(2 * cols + (k + 1) * lanes, lanes)
            sums_out[:, at] = jnp.sum(jnp.where(diagonal(rows), values, 0.0), axis=0, keepdims=True)
        for k in range(cols // lanes):
            at = pl.ds(k * lanes, lanes)
            values = grad_ref[:, at]
            put(at, col_ref[:, at])
            put(pl.ds(cols + k * lanes, lanes), jnp.sum(values * values * inverse, axis=0, keepdims=True))
        for half in refs[len(row_parts) + len(held) : len(row_parts) + len(held) + len(halves)]:
            side = lax.rem(lax.axis_index("row"), 2)
            for k in range(cols // 2 // lanes):
                sums_out[:, half_of(side, cols, k)] += half[:, pl.ds(k * lanes, lanes)]
                sums_out[:, half_of(side + 2, cols, k)] += half[:, pl.ds(cols // 2 + k * lanes, lanes)]
            sums_out[:, pl.ds(2 * cols, lanes)] += half[:, pl.ds(cols, lanes)]

    return pl.pallas_call(
        body,
        out_shape=(f32(rows, lanes), f32(1, 2 * cols + (1 + len(carried)) * lanes)),
        in_specs=[ON_CHIP] * (3 + len(row_parts) + len(held) + len(halves) + len(carried)),
        out_specs=(ON_CHIP, ON_CHIP),
        compiler_params=limits,
        cost_estimate=cost(rows * cols, 4, 4),
        name="scale",
    )(gradient, col_part, old_rows, *row_parts, *held, *halves, *carried)


def column_factor(sums, extra, old_cols, matrix_rows):
    cols = old_cols.shape[1]

    def body(sums_ref, old_ref, *refs):
        col_out, scale_out, update_out, mean_out = refs[-4:]
        weight = 1.0
        if extra:
            place = lax.axis_index("dp")
            ends = jnp.logical_or(place == 0, place == lax.axis_size("dp") - 1)
            weight = jnp.where(ends, 0.0, 1.0)

        def total(at):
            value = sums_ref[:, at]
            if extra:
                value = value * weight
            for ref in refs[: len(extra)]:
                value = value + ref[:, at]
            return value

        col = beta_two * old_ref[...] + (1.0 - beta_two) * (total(pl.ds(0, cols)) / matrix_rows)
        col_out[...] = col
        scale_out[...] = lax.rsqrt(col)
        ratio = total(pl.ds(cols, cols)) / col
        update = ratio[:, :lanes]
        for k in range(1, cols // lanes):
            update = update + ratio[:, k * lanes : (k + 1) * lanes]
        update_out[...] = update
        mean_out[...] = total(pl.ds(2 * cols, lanes)) / matrix_rows

    return pl.pallas_call(
        body,
        out_shape=(f32(1, cols), f32(1, cols), f32(1, lanes), f32(1, lanes)),
        in_specs=[ON_CHIP] * (2 + len(extra)),
        out_specs=(ON_CHIP,) * 4,
        compiler_params=limits,
        cost_estimate=cost(cols, 4, 12),
        name="columns",
    )(sums, old_cols, *extra)


def select_run(choices, action):
    place = lax.axis_index("dp")
    for c, (places, _, _) in enumerate(choices):
        if len(choices) == 1:
            action(c)
        else:
            chosen = place == places[0]
            for other in places[1:]:
                chosen = jnp.logical_or(chosen, place == other)
            pl.when(chosen)(lambda c=c: action(c))


def apply_first(weights, choices, col_scale, row_mean, updates, matrix_rows, hidden_width):
    pieces = len(choices[0][1])
    count = pieces - 1
    rows, cols = choices[0][1][0].shape
    arrays = [array for _, gradient, new_row in choices for array in (*gradient[:count], *new_row)]
    each = count + pieces

    def body(weights_ref, col_ref, mean_ref, *refs):
        update_refs = refs[len(arrays) : len(arrays) + len(updates)]
        out_ref, factor_ref, scale_ref, held, sems = refs[-5:]
        update_total = update_refs[0][...]
        for ref in update_refs[1:]:
            update_total = update_total + ref[...]
        update_total = jnp.sum(update_total, axis=1, keepdims=True)
        row_mean = mean_ref[:, :1]
        clip_ratio = jnp.sqrt(update_total * row_mean / (matrix_rows * hidden_width))
        factor = step_rate * jnp.sqrt(row_mean) / jnp.maximum(1.0, clip_ratio)
        col_factor = factor * col_ref[...]
        factor_ref[...] = col_factor

        def copy(k):
            here = pl.ds(k * rows, rows)
            return pltpu.make_async_copy(held.at[here, :], out_ref.at[here, :], sems.at[k])

        for k in range(count):

            def write(c, k=k):
                here = pl.ds(k * rows, rows)
                row_scale = lax.rsqrt(refs[c * each + count + k][:, :1])
                held[here, :] = weights_ref[here, :] - refs[c * each + k][...] * row_scale * col_factor

            select_run(choices, write)
            copy(k).start()

        def last_scale(c):
            scale_ref[...] = lax.rsqrt(refs[c * each + count + pieces - 1][...])

        select_run(choices, last_scale)
        for k in range(count):
            copy(k).wait()

    return pl.pallas_call(
        body,
        out_shape=(f32(rows * pieces, cols), f32(1, cols), f32(rows, lanes)),
        in_specs=[ON_CHIP] * (3 + len(arrays) + len(updates)),
        out_specs=(IN_PLACE, ON_CHIP, ON_CHIP),
        scratch_shapes=[pltpu.VMEM((rows * count, cols), jnp.float32), pltpu.SemaphoreType.DMA((count,))],
        compiler_params=limits,
        cost_estimate=cost(rows * count * cols, 4, 12),
        name="apply",
    )(weights, col_scale, row_mean, *arrays, *updates)


def apply_last(weights, choices, begun, col_factor, row_scale):
    pieces = len(choices[0][1])
    rows, cols = choices[0][1][0].shape
    chunk = min(rows, 8)
    first = (pieces - 1) * rows
    arrays = [gradient[-1] for _, gradient, _ in choices]

    def body(weights_ref, factor_ref, scale_ref, *refs):
        out_ref, held, sems = refs[-3:]

        def copy(k):
            here = held.at[pl.ds(k * chunk, chunk), :]
            return pltpu.make_async_copy(here, out_ref.at[pl.ds(first + k * chunk, chunk), :], sems.at[k])

        def write(c):
            for k in range(rows // chunk):
                here = pl.ds(k * chunk, chunk)
                step = refs[c][here, :] * scale_ref[here, :1] * factor_ref[...]
                held[here, :] = weights_ref[first + k * chunk : first + (k + 1) * chunk, :] - step
                copy(k).start()

        select_run(choices, write)
        for k in range(rows // chunk):
            copy(k).wait()

    return pl.pallas_call(
        body,
        out_shape=f32(rows * pieces, cols),
        in_specs=[ON_CHIP] * (3 + len(arrays)) + [IN_PLACE],
        out_specs=IN_PLACE,
        scratch_shapes=[pltpu.VMEM((rows, cols), jnp.float32), pltpu.SemaphoreType.DMA((rows // chunk,))],
        input_output_aliases={3 + len(arrays): 0},
        compiler_params=limits,
        cost_estimate=cost(rows * cols, 3, 12),
        name="last",
    )(weights, col_factor, row_scale, *arrays, begun)


def row_line(choices):
    count = len(choices[0][2])
    rows = choices[0][2][0].shape[0]
    arrays = [array for _, _, new_row in choices for array in new_row]

    def body(*refs):
        place = lax.axis_index("dp")
        row = lax.broadcasted_iota(jnp.int32, (rows, lanes), 0)
        lane = lax.broadcasted_iota(jnp.int32, (rows, lanes), 1)
        line = jnp.zeros((1, lanes), jnp.float32)
        for piece in range(count):
            values = refs[piece][...]
            for c, (places, _, _) in enumerate(choices[1:], 1):
                for other in places:
                    values = jnp.where(place == other, refs[c * count + piece][...], values)
            at = lane == row + piece * rows
            line = line + jnp.sum(jnp.where(at, values, 0.0), axis=0, keepdims=True)
        refs[-1][...] = line

    return pl.pallas_call(
        body,
        out_shape=f32(1, lanes),
        in_specs=[ON_CHIP] * len(arrays),
        out_specs=ON_CHIP,
        compiler_params=limits,
        cost_estimate=cost(rows * count * lanes, 2, 4),
        name="rows",
    )(*arrays)


def short_line(grad, old_rows, hidden_width, pieces, rows):
    last = 3
    late = range(pieces // 2, pieces)
    soon = range(pieces // 2)
    order = [(2, p) for p in late] + [(3, p) for p in range(pieces)] + [(2, p) for p in soon]
    order += [(1, p) for p in soon] + [(1, p) for p in late]
    swap = [(0, 1), (1, 0), (2, 3), (3, 2)]
    middle = [(1, 2), (2, 1)]
    outward = [(0, 1), (3, 2)]
    ends = [0, last]

    def right(m):
        shard, piece = order[min(max(m, 0), len(order) - 1)]
        return shard * pieces + piece

    def left(m):
        shard, piece = order[min(max(m, 0), len(order) - 1)]
        return (last - shard) * pieces + piece

    P, M = {}, {}
    finished, new_row = {}, {}
    sums = []

    def own_table(slot):
        return [left(slot - 3), right(slot), left(slot), right(slot - 3)]

    def settle(slot, extra=()):
        table = own_table(slot)
        counted = [int(slot <= 8), int(slot >= 8), int(slot >= 8), int(slot <= 8)]
        arrived = [P[slot], M[slot]] if slot >= 8 else [P[slot]]
        gradient, row_part, col_part = finish_block(staged, table, arrived, rows)
        row_parts = [row_part] + other_parts(row_part, "col")
        finished[slot] = gradient
        carried = [new_row[3], new_row[4]] if slot == 8 else []
        new_row[slot], total = scale_block(
            gradient, table, counted, row_parts, old_rows, col_part, sums[-1:], list(extra), carried, hidden_width
        )
        sums.append(total)

    for slot in range(10):
        if slot >= 2:
            operand = block_sum(staged, [0, right(slot - 2), left(slot - 2), 0], [P[slot - 2]], [], rows)
            M[slot] = lax.ppermute(operand, "dp", middle)
        table = [right(slot), left(slot - 3), right(slot - 3), left(slot)]
        arrived = [M[slot - 1]] if slot >= 3 else []
        if slot < 2:
            operand = fetch_block(grad, table, [1, 0, 0, 1], rows)
            staged = stage_gradient(grad, [operand])
        else:
            tokens = [P[0]] if slot == 2 else sums[-2:-1]
            operand = block_sum(staged, table, arrived, tokens, rows)
        P[slot] = lax.ppermute(operand, "dp", outward if slot in (1, 2) else swap)
        if 3 <= slot <= 8:
            settle(slot)
    cols = grad.shape[1]
    side = lax.axis_size("row")
    received = lax.ppermute(other_half(sums[-1], cols), "row", [(i, i ^ 1) for i in range(side)])
    early = lax.ppermute(joined_half(sums[-1], received, cols), "dp", outward)
    late_rows = unpack_rows(early, grad.shape[1], 2, rows)
    operand = pass_on(finished[3], [sums[-1]])
    P[10] = lax.ppermute(operand, "dp", outward)
    P[11] = lax.ppermute(pass_on(finished[4], [operand, early]), "dp", outward)
    settle(9, [early])
    total = axis_sum(sums[-1], "row")
    total = total + lax.ppermute(total, "dp", middle)
    extra = [lax.ppermute(total, "dp", [(1, 0), (2, 3)])]
    outer = ([finished[k] for k in range(5, 9)], [new_row[k] for k in range(5, 9)])
    inner = (
        [finished[8], finished[9], P[10], P[11]],
        [new_row[8], new_row[9], *late_rows],
    )
    return total, extra, [(ends, *outer), ([1, 2], *inner)]


def long_line(grad, old_rows, hidden_width, pieces, rows):
    replicas = lax.axis_size("dp")
    to_right = [(i, i + 1) for i in range(replicas - 1)]
    to_left = [(i + 1, i) for i in range(replicas - 1)]
    rights, lefts = {}, {}
    for slot in range((replicas - 1) * pieces):
        step, piece = divmod(slot, pieces)
        right_table = [min(replicas - 1 - step + z, replicas - 1) * pieces + piece for z in range(replicas)]
        left_table = [max(step - (replicas - 1) + z, 0) * pieces + piece for z in range(replicas)]
        before = slot - pieces
        right = block_sum(grad, right_table, [rights[before]] if step else [], [], rows)
        left = block_sum(grad, left_table, [lefts[before]] if step else [], [], rows)
        rights[slot] = lax.ppermute(right, "dp", to_right[: step + 1])
        lefts[slot] = lax.ppermute(left, "dp", to_left[replicas - 2 - step :])
    gradient, new_row, held = [], [], []
    for piece in range(pieces):
        slot = (replicas - 2) * pieces + piece
        table = [z * pieces + piece for z in range(replicas)]
        grad_piece, row_part, col_part = finish_block(grad, table, [rights[slot], lefts[slot]], rows)
        row_parts = [row_part] + other_parts(row_part, "col")
        row_piece, sums = scale_block(
            grad_piece, table, [1] * replicas, row_parts, old_rows, col_part, held, [], [], hidden_width
        )
        held = [sums]
        gradient.append(grad_piece)
        new_row.append(row_piece)
    total = axis_sum(axis_sum(sums, "row"), "dp")
    return total, [], [(list(range(replicas)), gradient, new_row)]


def shards(grad_parts, params, row_second, col_second):
    owned_rows = params.shape[2]
    local_cols = params.shape[3]
    slab_rows = row_second.shape[2]
    hidden_width = local_cols * lax.axis_size("col")
    matrix_rows = slab_rows * lax.axis_size("row")
    replicas = lax.axis_size("dp")
    pieces = 4 if owned_rows >= 64 else 2
    rows = owned_rows // pieces
    grad = grad_parts.reshape(slab_rows, local_cols)
    weights = params.reshape(owned_rows, local_cols)
    old_rows = jnp.broadcast_to(row_second.reshape(slab_rows, 1), (slab_rows, lanes))
    old_cols = col_second.reshape(1, local_cols)
    short = replicas == 4 and pieces == 4 and lax.axis_size("row") % 2 == 0 and local_cols % (2 * lanes) == 0
    line = short_line if short else long_line
    total, extra, choices = line(grad, old_rows, hidden_width, pieces, rows)
    new_col, col_scale, update_part, row_mean = column_factor(total, extra, old_cols, matrix_rows)
    updates = [update_part] + other_parts(update_part, "col")
    begun, col_factor, row_scale = apply_first(
        weights, choices, col_scale, row_mean, updates, matrix_rows, hidden_width
    )
    new_params = apply_last(weights, choices, begun, col_factor, row_scale)
    new_row = row_line(choices)[:, :owned_rows]
    return (new_params.reshape(params.shape), new_row.reshape(1, 1, owned_rows), new_col)


def solution(mesh):
    return jax.shard_map(
        shards,
        mesh=mesh,
        in_specs=(
            P("dp", None, "row", None, "col"),
            P(None, "row", "dp", "col"),
            P(None, "row", None),
            P(None, "col"),
        ),
        out_specs=(P(None, "row", "dp", "col"), P(None, "row", "dp"), P(None, "col")),
        check_vma=False,
    )
```

```python
import jax
import jax.numpy as jnp
from jax import lax
from jax.experimental import pallas as pl
from jax.experimental.pallas import tpu as pltpu
from jax.sharding import PartitionSpec as P

beta_two = 1.0 - 8.0 ** (-0.8)
step_rate = 0.5
tiny_add = 1e-30
lanes = 128
ON_CHIP = pl.BlockSpec(memory_space=pltpu.VMEM)
IN_PLACE = pl.BlockSpec(memory_space=pltpu.HBM)
limits = pltpu.CompilerParams(vmem_limit_bytes=8 * 1024 * 1024)


def f32(*shape):
    return jax.ShapeDtypeStruct(shape, jnp.float32)


def cost(elements, flops, width):
    return pl.CostEstimate(flops=flops * elements, bytes_accessed=width * elements, transcendentals=0)


def axis_sum(values, axis):
    size = lax.axis_size(axis)
    hop = 1
    while hop < size:
        pairs = [(i, i ^ hop) for i in range(size)]
        values = values + lax.ppermute(values, axis, pairs)
        hop *= 2
    return values


def other_parts(values, axis):
    size = lax.axis_size(axis)
    return [lax.ppermute(values, axis, [(i, (i + k) % size) for i in range(size)]) for k in range(1, size)]


def pick(table):
    place = lax.axis_index("dp")
    value = jnp.int32(table[0])
    for k in range(1, len(table)):
        value = jnp.where(place == k, jnp.int32(table[k]), value)
    return value


def block_sum(grad, table, arrived, tokens, rows):
    cols = grad.shape[1]

    def body(grad_ref, *refs):
        start = pl.multiple_of(pick(table) * rows, rows)
        values = grad_ref[pl.ds(start, rows), :].astype(jnp.float32)
        for ref in refs[: len(arrived)]:
            values = values + ref[...]
        refs[-1][...] = values

    return pl.pallas_call(
        body,
        out_shape=f32(rows, cols),
        in_specs=[ON_CHIP] * (1 + len(arrived) + len(tokens)),
        out_specs=ON_CHIP,
        compiler_params=limits,
        cost_estimate=cost(rows * cols, 1, 10),
        name="block",
    )(grad, *arrived, *tokens)


def stage_gradient(grad, tokens):
    def body(grad_ref, *refs):
        out_ref, sem = refs[-2:]
        copy = pltpu.make_async_copy(grad_ref, out_ref, sem)
        copy.start()
        copy.wait()

    return pl.pallas_call(
        body,
        out_shape=jax.ShapeDtypeStruct(grad.shape, grad.dtype),
        in_specs=[IN_PLACE] + [ON_CHIP] * len(tokens),
        out_specs=ON_CHIP,
        scratch_shapes=[pltpu.SemaphoreType.DMA(())],
        compiler_params=limits,
        cost_estimate=cost(grad.size, 0, 2),
        name="stage",
    )(pltpu.with_memory_space_constraint(grad, pltpu.HBM), *tokens)


def fetch_block(grad, table, places, rows):
    cols = grad.shape[1]
    chunk = min(rows, 8)

    def body(grad_ref, out_ref, held, sems):
        wanted = pick(places) > 0
        start = pick(table) * rows

        def copy(k):
            at = pl.ds(pl.multiple_of(start + k * chunk, chunk), chunk)
            return pltpu.make_async_copy(grad_ref.at[at, :], held.at[pl.ds(k * chunk, chunk), :], sems.at[k])

        @pl.when(wanted)
        def _():
            for k in range(rows // chunk):
                copy(k).start()
            for k in range(rows // chunk):
                at = pl.ds(k * chunk, chunk)
                copy(k).wait()
                out_ref[at, :] = held[at, :].astype(jnp.float32)

        @pl.when(jnp.logical_not(wanted))
        def _():
            out_ref[...] = jnp.zeros((rows, cols), jnp.float32)

    return pl.pallas_call(
        body,
        out_shape=f32(rows, cols),
        in_specs=[IN_PLACE],
        out_specs=ON_CHIP,
        scratch_shapes=[pltpu.VMEM((rows, cols), grad.dtype), pltpu.SemaphoreType.DMA((rows // chunk,))],
        compiler_params=limits,
        cost_estimate=cost(rows * cols, 1, 6),
        name="fetch",
    )(pltpu.with_memory_space_constraint(grad, pltpu.HBM))


def pass_on(values, tokens):
    def body(values_ref, *refs):
        refs[-1][...] = values_ref[...]

    return pl.pallas_call(
        body,
        out_shape=f32(*values.shape),
        in_specs=[ON_CHIP] * (1 + len(tokens)),
        out_specs=ON_CHIP,
        compiler_params=limits,
        cost_estimate=cost(values.size, 1, 8),
        name="pass",
    )(values, *tokens)


def finish_block(grad, table, arrived, rows):
    cols = arrived[0].shape[1]

    def body(grad_ref, *refs):
        out_ref, row_ref, col_ref = refs[-3:]
        start = pl.multiple_of(pick(table) * rows, rows)
        for k in range(cols // lanes):
            at = pl.ds(k * lanes, lanes)
            values = grad_ref[pl.ds(start, rows), at].astype(jnp.float32)
            for ref in refs[: len(arrived)]:
                values = values + ref[:, at]
            out_ref[:, at] = values
            squares = values * values + tiny_add
            row_part = squares if k == 0 else row_part + squares
            col_ref[:, at] = jnp.sum(squares, axis=0, keepdims=True)
        row_ref[...] = row_part

    return pl.pallas_call(
        body,
        out_shape=(f32(rows, cols), f32(rows, lanes), f32(1, cols)),
        in_specs=[ON_CHIP] * (1 + len(arrived)),
        out_specs=(ON_CHIP,) * 3,
        compiler_params=limits,
        cost_estimate=cost(rows * cols, 6, 14),
        name="finish",
    )(grad, *arrived)


def diagonal(rows):
    row = lax.broadcasted_iota(jnp.int32, (rows, lanes), 0)
    return row == lax.broadcasted_iota(jnp.int32, (rows, lanes), 1)


def half_of(side, cols, k):
    return pl.ds(pl.multiple_of(side * (cols // 2) + k * lanes, lanes), lanes)


def other_half(sums, cols):
    def body(sums_ref, out_ref):
        side = 1 - lax.rem(lax.axis_index("row"), 2)
        for k in range(cols // 2 // lanes):
            out_ref[:, pl.ds(k * lanes, lanes)] = sums_ref[:, half_of(side, cols, k)]
            out_ref[:, pl.ds(cols // 2 + k * lanes, lanes)] = sums_ref[:, half_of(side + 2, cols, k)]

    return pl.pallas_call(
        body,
        out_shape=f32(1, cols),
        in_specs=[ON_CHIP],
        out_specs=ON_CHIP,
        compiler_params=limits,
        cost_estimate=cost(cols, 1, 8),
        name="half",
    )(sums)


def joined_half(sums, received, cols):
    width = sums.shape[1] - cols

    def body(sums_ref, received_ref, out_ref):
        side = lax.rem(lax.axis_index("row"), 2)
        for k in range(cols // 2 // lanes):
            at = pl.ds(k * lanes, lanes)
            out_ref[:, at] = sums_ref[:, half_of(side, cols, k)] + received_ref[:, at]
            at = pl.ds(cols // 2 + k * lanes, lanes)
            out_ref[:, at] = sums_ref[:, half_of(side + 2, cols, k)] + received_ref[:, at]
        out_ref[:, cols:width] = sums_ref[:, 2 * cols : cols + width]

    return pl.pallas_call(
        body,
        out_shape=f32(1, width),
        in_specs=[ON_CHIP] * 2,
        out_specs=ON_CHIP,
        compiler_params=limits,
        cost_estimate=cost(cols, 1, 12),
        name="joined",
    )(sums, received)


def unpack_rows(sums, cols, count, rows):
    def body(sums_ref, *outs):
        for k, out in enumerate(outs):
            values = sums_ref[:, pl.ds(cols + (k + 1) * lanes, lanes)]
            column = jnp.sum(jnp.where(diagonal(rows), values, 0.0), axis=1, keepdims=True)
            out[...] = jnp.broadcast_to(column, (rows, lanes))

    return pl.pallas_call(
        body,
        out_shape=(f32(rows, lanes),) * count,
        in_specs=[ON_CHIP],
        out_specs=(ON_CHIP,) * count,
        compiler_params=limits,
        cost_estimate=cost(rows * lanes, 2, 8),
        name="unpack",
    )(sums)


def scale_block(gradient, table, counted, row_parts, old_rows, col_part, held, halves, carried, hidden_width):
    rows, cols = gradient.shape

    def body(grad_ref, col_ref, old_ref, *refs):
        row_out, sums_out = refs[-2:]
        total = refs[0][...]
        for ref in refs[1 : len(row_parts)]:
            total = total + ref[...]
        row_sum = jnp.sum(total, axis=1, keepdims=True)
        old = old_ref[pl.ds(pl.multiple_of(pick(table) * rows, rows), rows), :]
        row = beta_two * old + (1.0 - beta_two) * (row_sum / hidden_width)
        row_out[...] = row
        inverse = 1.0 / row
        before = refs[len(row_parts) : len(row_parts) + len(held)]
        counts = pick(counted) > 0

        def put(at, value):
            value = jnp.where(counts, value, 0.0)
            for ref in before:
                value = value + ref[:, at]
            sums_out[:, at] = value

        put(pl.ds(2 * cols, lanes), jnp.sum(row, axis=0, keepdims=True))
        for k in range(len(carried)):
            values = refs[len(row_parts) + len(held) + len(halves) + k][...]
            at = pl.ds(2 * cols + (k + 1) * lanes, lanes)
            sums_out[:, at] = jnp.sum(jnp.where(diagonal(rows), values, 0.0), axis=0, keepdims=True)
        for k in range(cols // lanes):
            at = pl.ds(k * lanes, lanes)
            values = grad_ref[:, at]
            put(at, col_ref[:, at])
            put(pl.ds(cols + k * lanes, lanes), jnp.sum(values * values * inverse, axis=0, keepdims=True))
        for half in refs[len(row_parts) + len(held) : len(row_parts) + len(held) + len(halves)]:
            side = lax.rem(lax.axis_index("row"), 2)
            for k in range(cols // 2 // lanes):
                sums_out[:, half_of(side, cols, k)] += half[:, pl.ds(k * lanes, lanes)]
                sums_out[:, half_of(side + 2, cols, k)] += half[:, pl.ds(cols // 2 + k * lanes, lanes)]
            sums_out[:, pl.ds(2 * cols, lanes)] += half[:, pl.ds(cols, lanes)]

    return pl.pallas_call(
        body,
        out_shape=(f32(rows, lanes), f32(1, 2 * cols + (1 + len(carried)) * lanes)),
        in_specs=[ON_CHIP] * (3 + len(row_parts) + len(held) + len(halves) + len(carried)),
        out_specs=(ON_CHIP, ON_CHIP),
        compiler_params=limits,
        cost_estimate=cost(rows * cols, 4, 4),
        name="scale",
    )(gradient, col_part, old_rows, *row_parts, *held, *halves, *carried)


def column_factor(sums, extra, old_cols, matrix_rows):
    cols = old_cols.shape[1]

    def body(sums_ref, old_ref, *refs):
        col_out, scale_out, update_out, mean_out = refs[-4:]
        weight = 1.0
        if extra:
            place = lax.axis_index("dp")
            ends = jnp.logical_or(place == 0, place == lax.axis_size("dp") - 1)
            weight = jnp.where(ends, 0.0, 1.0)

        def total(at):
            value = sums_ref[:, at]
            if extra:
                value = value * weight
            for ref in refs[: len(extra)]:
                value = value + ref[:, at]
            return value

        col = beta_two * old_ref[...] + (1.0 - beta_two) * (total(pl.ds(0, cols)) / matrix_rows)
        col_out[...] = col
        scale_out[...] = lax.rsqrt(col)
        ratio = total(pl.ds(cols, cols)) / col
        update = ratio[:, :lanes]
        for k in range(1, cols // lanes):
            update = update + ratio[:, k * lanes : (k + 1) * lanes]
        update_out[...] = update
        mean_out[...] = total(pl.ds(2 * cols, lanes)) / matrix_rows

    return pl.pallas_call(
        body,
        out_shape=(f32(1, cols), f32(1, cols), f32(1, lanes), f32(1, lanes)),
        in_specs=[ON_CHIP] * (2 + len(extra)),
        out_specs=(ON_CHIP,) * 4,
        compiler_params=limits,
        cost_estimate=cost(cols, 4, 12),
        name="columns",
    )(sums, old_cols, *extra)


def select_run(choices, action):
    place = lax.axis_index("dp")
    for c, (places, _, _) in enumerate(choices):
        if len(choices) == 1:
            action(c)
        else:
            chosen = place == places[0]
            for other in places[1:]:
                chosen = jnp.logical_or(chosen, place == other)
            pl.when(chosen)(lambda c=c: action(c))


def apply_first(weights, choices, col_scale, row_mean, updates, matrix_rows, hidden_width):
    pieces = len(choices[0][1])
    count = pieces - 1
    rows, cols = choices[0][1][0].shape
    arrays = [array for _, gradient, new_row in choices for array in (*gradient[:count], *new_row)]
    each = count + pieces

    def body(weights_ref, col_ref, mean_ref, *refs):
        update_refs = refs[len(arrays) : len(arrays) + len(updates)]
        out_ref, factor_ref, scale_ref, held, sems = refs[-5:]
        update_total = update_refs[0][...]
        for ref in update_refs[1:]:
            update_total = update_total + ref[...]
        update_total = jnp.sum(update_total, axis=1, keepdims=True)
        row_mean = mean_ref[:, :1]
        clip_ratio = jnp.sqrt(update_total * row_mean / (matrix_rows * hidden_width))
        factor = step_rate * jnp.sqrt(row_mean) / jnp.maximum(1.0, clip_ratio)
        col_factor = factor * col_ref[...]
        factor_ref[...] = col_factor

        def copy(k):
            here = pl.ds(k * rows, rows)
            return pltpu.make_async_copy(held.at[here, :], out_ref.at[here, :], sems.at[k])

        for k in range(count):

            def write(c, k=k):
                here = pl.ds(k * rows, rows)
                row_scale = lax.rsqrt(refs[c * each + count + k][:, :1])
                held[here, :] = weights_ref[here, :] - refs[c * each + k][...] * row_scale * col_factor

            select_run(choices, write)
            copy(k).start()

        def last_scale(c):
            scale_ref[...] = lax.rsqrt(refs[c * each + count + pieces - 1][...])

        select_run(choices, last_scale)
        for k in range(count):
            copy(k).wait()

    return pl.pallas_call(
        body,
        out_shape=(f32(rows * pieces, cols), f32(1, cols), f32(rows, lanes)),
        in_specs=[ON_CHIP] * (3 + len(arrays) + len(updates)),
        out_specs=(IN_PLACE, ON_CHIP, ON_CHIP),
        scratch_shapes=[pltpu.VMEM((rows * count, cols), jnp.float32), pltpu.SemaphoreType.DMA((count,))],
        compiler_params=limits,
        cost_estimate=cost(rows * count * cols, 4, 12),
        name="apply",
    )(weights, col_scale, row_mean, *arrays, *updates)


def apply_last(weights, choices, begun, col_factor, row_scale):
    pieces = len(choices[0][1])
    rows, cols = choices[0][1][0].shape
    chunk = min(rows, 8)
    first = (pieces - 1) * rows
    arrays = [gradient[-1] for _, gradient, _ in choices]

    def body(weights_ref, factor_ref, scale_ref, *refs):
        out_ref, held, sems = refs[-3:]

        def copy(k):
            here = held.at[pl.ds(k * chunk, chunk), :]
            return pltpu.make_async_copy(here, out_ref.at[pl.ds(first + k * chunk, chunk), :], sems.at[k])

        def write(c):
            for k in range(rows // chunk):
                here = pl.ds(k * chunk, chunk)
                step = refs[c][here, :] * scale_ref[here, :1] * factor_ref[...]
                held[here, :] = weights_ref[first + k * chunk : first + (k + 1) * chunk, :] - step
                copy(k).start()

        select_run(choices, write)
        for k in range(rows // chunk):
            copy(k).wait()

    return pl.pallas_call(
        body,
        out_shape=f32(rows * pieces, cols),
        in_specs=[ON_CHIP] * (3 + len(arrays)) + [IN_PLACE],
        out_specs=IN_PLACE,
        scratch_shapes=[pltpu.VMEM((rows, cols), jnp.float32), pltpu.SemaphoreType.DMA((rows // chunk,))],
        input_output_aliases={3 + len(arrays): 0},
        compiler_params=limits,
        cost_estimate=cost(rows * cols, 3, 12),
        name="last",
    )(weights, col_factor, row_scale, *arrays, begun)


def row_line(choices):
    count = len(choices[0][2])
    rows = choices[0][2][0].shape[0]
    arrays = [array for _, _, new_row in choices for array in new_row]

    def body(*refs):
        place = lax.axis_index("dp")
        row = lax.broadcasted_iota(jnp.int32, (rows, lanes), 0)
        lane = lax.broadcasted_iota(jnp.int32, (rows, lanes), 1)
        line = jnp.zeros((1, lanes), jnp.float32)
        for piece in range(count):
            values = refs[piece][...]
            for c, (places, _, _) in enumerate(choices[1:], 1):
                for other in places:
                    values = jnp.where(place == other, refs[c * count + piece][...], values)
            at = lane == row + piece * rows
            line = line + jnp.sum(jnp.where(at, values, 0.0), axis=0, keepdims=True)
        refs[-1][...] = line

    return pl.pallas_call(
        body,
        out_shape=f32(1, lanes),
        in_specs=[ON_CHIP] * len(arrays),
        out_specs=ON_CHIP,
        compiler_params=limits,
        cost_estimate=cost(rows * count * lanes, 2, 4),
        name="rows",
    )(*arrays)


def short_line(grad, old_rows, hidden_width, pieces, rows):
    last = 3
    late = range(pieces // 2, pieces)
    soon = range(pieces // 2)
    order = [(2, p) for p in late] + [(3, p) for p in range(pieces)] + [(2, p) for p in soon]
    order += [(1, p) for p in soon] + [(1, p) for p in late]
    swap = [(0, 1), (1, 0), (2, 3), (3, 2)]
    middle = [(1, 2), (2, 1)]
    outward = [(0, 1), (3, 2)]
    ends = [0, last]

    def right(m):
        shard, piece = order[min(max(m, 0), len(order) - 1)]
        return shard * pieces + piece

    def left(m):
        shard, piece = order[min(max(m, 0), len(order) - 1)]
        return (last - shard) * pieces + piece

    P, M = {}, {}
    finished, new_row = {}, {}
    sums = []

    def own_table(slot):
        return [left(slot - 3), right(slot), left(slot), right(slot - 3)]

    def settle(slot, extra=()):
        table = own_table(slot)
        counted = [int(slot <= 8), int(slot >= 8), int(slot >= 8), int(slot <= 8)]
        arrived = [P[slot], M[slot]] if slot >= 8 else [P[slot]]
        gradient, row_part, col_part = finish_block(staged, table, arrived, rows)
        row_parts = [row_part] + other_parts(row_part, "col")
        finished[slot] = gradient
        carried = [new_row[3], new_row[4]] if slot == 8 else []
        new_row[slot], total = scale_block(
            gradient, table, counted, row_parts, old_rows, col_part, sums[-1:], list(extra), carried, hidden_width
        )
        sums.append(total)

    for slot in range(10):
        if slot >= 2:
            operand = block_sum(staged, [0, right(slot - 2), left(slot - 2), 0], [P[slot - 2]], [], rows)
            M[slot] = lax.ppermute(operand, "dp", middle)
        table = [right(slot), left(slot - 3), right(slot - 3), left(slot)]
        arrived = [M[slot - 1]] if slot >= 3 else []
        if slot < 2:
            operand = fetch_block(grad, table, [1, 0, 0, 1], rows)
            staged = stage_gradient(grad, [operand])
        else:
            tokens = [P[0]] if slot == 2 else sums[-2:-1]
            operand = block_sum(staged, table, arrived, tokens, rows)
        P[slot] = lax.ppermute(operand, "dp", outward if slot in (1, 2, 9) else swap)
        if 3 <= slot <= 8:
            settle(slot)
    cols = grad.shape[1]
    side = lax.axis_size("row")
    received = lax.ppermute(other_half(sums[-1], cols), "row", [(i, i ^ 1) for i in range(side)])
    early = lax.ppermute(joined_half(sums[-1], received, cols), "dp", outward)
    late_rows = unpack_rows(early, grad.shape[1], 2, rows)
    operand = pass_on(finished[3], [sums[-1]])
    P[10] = lax.ppermute(operand, "dp", outward)
    P[11] = lax.ppermute(pass_on(finished[4], [operand, early]), "dp", outward)
    settle(9, [early])
    total = axis_sum(sums[-1], "row")
    total = total + lax.ppermute(total, "dp", middle)
    extra = [lax.ppermute(total, "dp", [(1, 0), (2, 3)])]
    outer = ([finished[k] for k in range(5, 9)], [new_row[k] for k in range(5, 9)])
    inner = (
        [finished[8], finished[9], P[10], P[11]],
        [new_row[8], new_row[9], *late_rows],
    )
    return total, extra, [(ends, *outer), ([1, 2], *inner)]


def long_line(grad, old_rows, hidden_width, pieces, rows):
    replicas = lax.axis_size("dp")
    to_right = [(i, i + 1) for i in range(replicas - 1)]
    to_left = [(i + 1, i) for i in range(replicas - 1)]
    rights, lefts = {}, {}
    for slot in range((replicas - 1) * pieces):
        step, piece = divmod(slot, pieces)
        right_table = [min(replicas - 1 - step + z, replicas - 1) * pieces + piece for z in range(replicas)]
        left_table = [max(step - (replicas - 1) + z, 0) * pieces + piece for z in range(replicas)]
        before = slot - pieces
        right = block_sum(grad, right_table, [rights[before]] if step else [], [], rows)
        left = block_sum(grad, left_table, [lefts[before]] if step else [], [], rows)
        rights[slot] = lax.ppermute(right, "dp", to_right[: step + 1])
        lefts[slot] = lax.ppermute(left, "dp", to_left[replicas - 2 - step :])
    gradient, new_row, held = [], [], []
    for piece in range(pieces):
        slot = (replicas - 2) * pieces + piece
        table = [z * pieces + piece for z in range(replicas)]
        grad_piece, row_part, col_part = finish_block(grad, table, [rights[slot], lefts[slot]], rows)
        row_parts = [row_part] + other_parts(row_part, "col")
        row_piece, sums = scale_block(
            grad_piece, table, [1] * replicas, row_parts, old_rows, col_part, held, [], [], hidden_width
        )
        held = [sums]
        gradient.append(grad_piece)
        new_row.append(row_piece)
    total = axis_sum(axis_sum(sums, "row"), "dp")
    return total, [], [(list(range(replicas)), gradient, new_row)]


def shards(grad_parts, params, row_second, col_second):
    owned_rows = params.shape[2]
    local_cols = params.shape[3]
    slab_rows = row_second.shape[2]
    hidden_width = local_cols * lax.axis_size("col")
    matrix_rows = slab_rows * lax.axis_size("row")
    replicas = lax.axis_size("dp")
    pieces = 4 if owned_rows >= 64 else 2
    rows = owned_rows // pieces
    grad = grad_parts.reshape(slab_rows, local_cols)
    weights = params.reshape(owned_rows, local_cols)
    old_rows = jnp.broadcast_to(row_second.reshape(slab_rows, 1), (slab_rows, lanes))
    old_cols = col_second.reshape(1, local_cols)
    short = replicas == 4 and pieces == 4 and lax.axis_size("row") % 2 == 0 and local_cols % (2 * lanes) == 0
    line = short_line if short else long_line
    total, extra, choices = line(grad, old_rows, hidden_width, pieces, rows)
    new_col, col_scale, update_part, row_mean = column_factor(total, extra, old_cols, matrix_rows)
    updates = [update_part] + other_parts(update_part, "col")
    begun, col_factor, row_scale = apply_first(
        weights, choices, col_scale, row_mean, updates, matrix_rows, hidden_width
    )
    new_params = apply_last(weights, choices, begun, col_factor, row_scale)
    new_row = row_line(choices)[:, :owned_rows]
    return (new_params.reshape(params.shape), new_row.reshape(1, 1, owned_rows), new_col)


def solution(mesh):
    return jax.shard_map(
        shards,
        mesh=mesh,
        in_specs=(
            P("dp", None, "row", None, "col"),
            P(None, "row", "dp", "col"),
            P(None, "row", None),
            P(None, "col"),
        ),
        out_specs=(P(None, "row", "dp", "col"), P(None, "row", "dp"), P(None, "col")),
        check_vma=False,
    )
```
